512 devices in a mesh: tm: 32 (over z, x_hi, core), gz: 16 (over x_lo, y).
Axes of the slice: x: 4 (x_hi: 2, x_lo: 2; x = x_hi * 2 + x_lo), y: 8, z: 8, core: 2. Of those that a mesh axis runs over, the one named last changes fastest.
Arguments:
- c_states: float32 [32, 3, 64, 16, 256], P('tm', None, 'gz'), may hold values from -6 to 6
- velocity: float32 [3, 64, 16, 256], P(None, 'gz'), may hold values from -0.11 to 0.11
Outputs:
- updated: float32 [32, 3, 64, 16, 256], P('tm', None, 'gz')
The draws below stay inside these ranges and needn't reach their ends.
All inputs are finite; a program needn't handle non-finite values.
Results may differ from the reference program's by a relative error of at most 0.00002.
Values sent between devices are 32-bit elements; how exact they have to be, the bound alone decides.
No kernel may reach another device: no remote copies, remote signals or barrier semaphores. Data moves between devices by JAX's collectives and lax.ppermute only.
A program may use at most 64 MiB of HBM per device.

```python
import jax
import jax.numpy as jnp
from jax import lax

X_CELLS = 16
Y_CELLS = 256
STEPS = 4
NZ = 64
INTERVALS = 32


def level_of(own_key, extent, pieces, low, top_value):
    loudness = 1.0
    for dim, parts in pieces:
        draws = jax.random.uniform(jax.random.fold_in(jax.random.fold_in(own_key, 6), dim), (parts,), jnp.float32, low / len(pieces), top_value / len(pieces))
        loudness = loudness * jnp.repeat(jnp.exp(draws), extent[dim] // parts).reshape((-1,) + (1,) * (len(extent) - 1 - dim))
    return loudness


def gaussian(own_key, dims, scale, reach, cuts=(), held_as=jnp.bfloat16):
    array = scale * jax.random.normal(own_key, dims, jnp.float32)
    if cuts:
        array = array * level_of(own_key, dims, cuts, -0.22, 0.18)
    return jnp.clip(array, -reach, reach).astype(held_as)


def setup_inputs(seed: int = 0) -> dict:
    arg_keys = jax.random.split(jax.random.key(seed), 3)
    c_states = gaussian(arg_keys[0], (INTERVALS, 3, NZ, X_CELLS, Y_CELLS), 1.0, 6.0, ((0, 32), (2, 16)), jnp.float32)
    velocity = jnp.clip(jax.random.uniform(arg_keys[1], (3, NZ, X_CELLS, Y_CELLS), jnp.float32, -0.11, 0.11) * level_of(arg_keys[1], (3, NZ, X_CELLS, Y_CELLS), ((1, 16),), -0.4, 0.0), -0.11, 0.11)
    return dict(c_states=c_states, velocity=velocity)


KAPPA = 0.04


def pad_space(values):
    return jnp.pad(values, ((0, 0), (1, 1), (1, 1), (1, 1)))


def neighbours(padded, direction):
    lower_cut = [slice(None), slice(1, -1), slice(1, -1), slice(1, -1)]
    upper_cut = list(lower_cut)
    lower_cut[direction] = slice(0, -2)
    upper_cut[direction] = slice(2, None)
    return padded[tuple(lower_cut)], padded[tuple(upper_cut)]


def tensor_of(courant):
    padded = pad_space(courant)
    columns = []
    for direction in (1, 2, 3):
        lower_side, upper_side = neighbours(padded, direction)
        columns.append((upper_side - lower_side) * 0.5)
    return jnp.stack(columns, axis=1)


def march_padded(padded, courant, tensor):
    middle = padded[:, 1:-1, 1:-1, 1:-1]
    advection = jnp.zeros_like(middle)
    laplace = jnp.zeros_like(middle)
    for direction in (1, 2, 3):
        lower_side, upper_side = neighbours(padded, direction)
        speed = courant[direction - 1][None]
        advection = advection + jnp.maximum(speed, 0.0) * (middle - lower_side) + jnp.minimum(speed, 0.0) * (upper_side - middle)
        laplace = laplace + upper_side + lower_side - 2.0 * middle
    stretch = tensor[:, 0] * middle[0:1] + tensor[:, 1] * middle[1:2] + tensor[:, 2] * middle[2:3]
    return middle - advection + stretch + KAPPA * laplace


def march(current, courant, tensor):
    return march_padded(pad_space(current), courant, tensor)


def coarsen(values):
    comps, zlen, xlen, ylen = values.shape
    return values.reshape(comps, zlen // 2, 2, xlen // 2, 2, ylen // 2, 2).mean(axis=(2, 4, 6))


def refine(values):
    return jnp.repeat(jnp.repeat(jnp.repeat(values, 2, 1), 2, 2), 2, 3)


def reference(c_states, velocity):
    tensor = tensor_of(velocity)
    coarse_speed = 2.0 * coarsen(velocity)
    coarse_tensor = tensor_of(coarse_speed)

    def propagate(start_state):
        current = start_state
        for _ in range(STEPS):
            current = march(current, velocity, tensor)
        return current

    stepped = lax.map(propagate, c_states)
    relaxed = jnp.concatenate([c_states[:1], stepped[:-1]], axis=0)
    again = lax.map(propagate, relaxed)
    coarse_relaxed = lax.map(coarsen, relaxed)
    coarse_again = lax.map(coarsen, again)

    def psi_of(field):
        return march(field, coarse_speed, coarse_tensor)

    forcing = coarse_again[:-1] - lax.map(psi_of, coarse_relaxed[:-1])

    def sweep(state, source):
        following = march(state, coarse_speed, coarse_tensor) + source
        return following, following

    first = coarse_relaxed[0]
    final_state, states = lax.scan(sweep, first, forcing)
    states = jnp.concatenate([first[None], states], axis=0)
    return relaxed + lax.map(refine, states - coarse_relaxed)
```

```python
import jax
import jax.numpy as jnp
from jax import lax
from jax.experimental import pallas as pl
from jax.experimental.pallas import tpu as pltpu
from jax.sharding import PartitionSpec as P

STEPS = 4
KAPPA = 0.04
F32 = jnp.float32
HI = lax.Precision.HIGHEST
VM = pltpu.MemorySpace.VMEM


def lane_parity(transpose=False):
    row = lax.broadcasted_iota(jnp.int32, (256, 256), 1 if transpose else 0)
    col = lax.broadcasted_iota(jnp.int32, (256, 256), 0 if transpose else 1)
    want = 2 * (col % 128) + col // 128
    return (row == want).astype(F32)


def shift(v, by, axis, masked_at, index):
    return jnp.where(index == masked_at, 0.0, pltpu.roll(v, by % v.shape[axis], axis))


def stencil_terms(low, high, mid, inside):
    a = [KAPPA + jnp.maximum(mid[d], 0.0) for d in range(3)]
    b = [KAPPA - jnp.minimum(mid[d], 0.0) for d in range(3)]
    centre = 1.0 - (a[0] + b[0] + a[1] + b[1] + a[2] + b[2])
    m = [[(high[e][c] - low[e][c]) * 0.5 for e in range(3)] for c in range(3)]
    for c in range(3):
        m[c][c] = m[c][c] + centre
    a = [x * inside for x in a]
    b = [x * inside for x in b]
    m = [[x * inside for x in row] for row in m]
    return a, b, m


def iotas():
    sub = lax.broadcasted_iota(jnp.int32, (8, 128), 0)
    lane = lax.broadcasted_iota(jnp.int32, (8, 128), 1)
    return sub, lane


def coarse_coefs(below, here, above, inside, store):
    sub, lane = iotas()
    low = [below, [shift(v, 1, 0, 0, sub) for v in here], [shift(v, 1, 1, 0, lane) for v in here]]
    high = [above, [shift(v, -1, 0, 7, sub) for v in here], [shift(v, -1, 1, 127, lane) for v in here]]
    a, b, m = stencil_terms(low, high, here, inside)
    a[1] = jnp.where(sub == 0, 0.0, a[1])
    b[1] = jnp.where(sub == 7, 0.0, b[1])
    a[2] = jnp.where(lane == 0, 0.0, a[2])
    b[2] = jnp.where(lane == 127, 0.0, b[2])
    flat = a + b + m[0] + m[1] + m[2]
    for i, x in enumerate(flat):
        store(i, x)


def psi(coef, below, here, above):
    a = [coef(i) for i in range(3)]
    b = [coef(3 + i) for i in range(3)]
    out = []
    for c in range(3):
        w = here[c]
        acc = a[0] * below[c] + b[0] * above[c]
        acc = acc + (a[1] * pltpu.roll(w, 1, 0) + b[1] * pltpu.roll(w, 7, 0))
        acc = acc + (a[2] * pltpu.roll(w, 1, 1) + b[2] * pltpu.roll(w, 127, 1))
        acc = acc + (coef(6 + 3 * c) * here[0] + coef(7 + 3 * c) * here[1] + coef(8 + 3 * c) * here[2])
        out.append(acc)
    return out


NL = 20


def fine_kernel(pos_ref, m2_ref, m1_ref, own_ref, p1_ref, p2_ref,
                start_ref, relaxed_ref, g_ref, first_ref, state_a, state_b, speed, coefs, ev, od):
    slab = pos_ref[0]
    anchor = pos_ref[1] == 1
    depth = pos_ref[2]
    perm = lane_parity()
    for i, ref in enumerate((m2_ref, m1_ref, own_ref, p1_ref, p2_ref)):
        z0 = 4 * i
        for part, dest in ((0, state_a), (1, speed)):
            rows = ref[3 * part:3 * part + 3].reshape(192, 256)
            both = jnp.dot(rows, perm, precision=HI, preferred_element_type=F32)
            ev[...] = both[:, :128]
            od[...] = both[:, 128:]
            for q in range(2):
                dest[:, z0:z0 + 4, 2 * q] = ev[pl.ds(q, 96, stride=2), :].reshape(3, 4, 8, 128)
                dest[:, z0:z0 + 4, 2 * q + 1] = od[pl.ds(q, 96, stride=2), :].reshape(3, 4, 8, 128)
    sub, lane = iotas()

    def build(l, carry):
        z = slab * 4 + l - 8
        inside = jnp.where(jnp.logical_and(z >= 0, z < depth), 1.0, 0.0).astype(F32)
        mid = [[speed[c, l, k] for c in range(3)] for k in range(4)]
        for q in range(2):
            for p in range(2):
                k = 2 * q + p
                here = mid[k]
                xo = mid[2 * (1 - q) + p]
                yo = mid[2 * q + 1 - p]
                low_z = [speed[c, l - 1, k] for c in range(3)]
                high_z = [speed[c, l + 1, k] for c in range(3)]
                low_x = xo if q else [shift(v, 1, 0, 0, sub) for v in xo]
                high_x = [shift(v, -1, 0, 7, sub) for v in xo] if q else xo
                low_y = yo if p else [shift(v, 1, 1, 0, lane) for v in yo]
                high_y = [shift(v, -1, 1, 127, lane) for v in yo] if p else yo
                a, b, m = stencil_terms([low_z, low_x, low_y], [high_z, high_x, high_y], here, inside)
                if q:
                    b[1] = jnp.where(sub == 7, 0.0, b[1])
                else:
                    a[1] = jnp.where(sub == 0, 0.0, a[1])
                if p:
                    b[2] = jnp.where(lane == 127, 0.0, b[2])
                else:
                    a[2] = jnp.where(lane == 0, 0.0, a[2])
                for i, x in enumerate(a + b + m[0] + m[1] + m[2]):
                    coefs[l, k, i] = x
        return carry

    lax.fori_loop(1, NL - 1, build, 0)

    def march(src, dst, first, last):
        def layer(l, carry):
            w = [[src[c, l, k] for k in range(4)] for c in range(3)]
            for q in range(2):
                for p in range(2):
                    k = 2 * q + p
                    kx = 2 * (1 - q) + p
                    ky = 2 * q + 1 - p
                    cf = [coefs[l, k, i] for i in range(15)]
                    for c in range(3):
                        xo = w[c][kx]
                        xr = pltpu.roll(xo, 7 if q else 1, 0)
                        yo = w[c][ky]
                        yr = pltpu.roll(yo, 127 if p else 1, 1)
                        acc = cf[0] * src[c, l - 1, k] + cf[3] * src[c, l + 1, k]
                        acc = acc + (cf[1] * (xo if q else xr) + cf[4] * (xr if q else xo))
                        acc = acc + (cf[2] * (yo if p else yr) + cf[5] * (yr if p else yo))
                        acc = acc + (cf[6 + 3 * c] * w[0][k] + cf[7 + 3 * c] * w[1][k] + cf[8 + 3 * c] * w[2][k])
                        dst[c, l, k] = acc
            return carry
        lax.fori_loop(first, last, layer, 0)

    def restrict(src, j):
        out = []
        for c in range(3):
            lo = (src[c, 2 * j, 0] + src[c, 2 * j, 1]) + (src[c, 2 * j, 2] + src[c, 2 * j, 3])
            hi = (src[c, 2 * j + 1, 0] + src[c, 2 * j + 1, 1]) + (src[c, 2 * j + 1, 2] + src[c, 2 * j + 1, 3])
            out.append((lo + hi) * 0.125)
        return out

    start_ref[...] = state_a[:, 8:12]
    coarse0 = {j: restrict(state_a, j) for j in range(2, 8)}
    speed_c = {j: [2.0 * v for v in restrict(speed, j)] for j in range(2, 8)}
    src, dst = state_a, state_b
    for k in range(1, 5):
        march(src, dst, k, NL - k)
        src, dst = dst, src
    relaxed_ref[...] = src[:, 8:12]
    coarse_r = {j: restrict(src, j) for j in range(3, 7)}
    for k in range(5, 9):
        march(src, dst, k, NL - k)
        src, dst = dst, src
    cc = {}
    for j in range(3, 7):
        z = slab * 2 + j - 4
        inside = jnp.where(jnp.logical_and(z >= 0, z < depth // 2), 1.0, 0.0).astype(F32)
        vals = {}
        coarse_coefs(speed_c[j - 1], speed_c[j], speed_c[j + 1], inside, vals.__setitem__)
        cc[j] = vals
    coarse1 = {}
    for j in range(3, 7):
        image = psi(cc[j].__getitem__, coarse0[j - 1], coarse0[j], coarse0[j + 1])
        coarse1[j] = [image[c] + (coarse_r[j][c] - image[c]) for c in range(3)]
    flag = jnp.where(anchor, 1.0, 0.0).astype(F32)
    for i, j in enumerate((4, 5)):
        again = restrict(src, j)
        image = psi(cc[j].__getitem__, coarse_r[j - 1], coarse_r[j], coarse_r[j + 1])
        start = psi(cc[j].__getitem__, coarse1[j - 1], coarse1[j], coarse1[j + 1])
        for c in range(3):
            forcing = again[c] - image[c]
            g_ref[c, i] = forcing + flag * start[c]
            first_ref[c, i] = coarse1[j][c]


def fine(pos, m2, m1, own, p1, p2):
    vm = pl.BlockSpec(memory_space=VM)
    return pl.pallas_call(
        fine_kernel,
        out_shape=(
            jax.ShapeDtypeStruct((3, 4, 4, 8, 128), F32),
            jax.ShapeDtypeStruct((3, 4, 4, 8, 128), F32),
            jax.ShapeDtypeStruct((3, 2, 8, 128), F32),
            jax.ShapeDtypeStruct((3, 2, 8, 128), F32),
        ),
        in_specs=[pl.BlockSpec(memory_space=pltpu.MemorySpace.SMEM)] + [vm] * 5,
        out_specs=(vm,) * 4,
        scratch_shapes=[
            pltpu.VMEM((3, NL, 4, 8, 128), F32),
            pltpu.VMEM((3, NL, 4, 8, 128), F32),
            pltpu.VMEM((3, NL, 4, 8, 128), F32),
            pltpu.VMEM((NL, 4, 15, 8, 128), F32),
            pltpu.VMEM((192, 128), F32),
            pltpu.VMEM((192, 128), F32),
        ],
        compiler_params=pltpu.CompilerParams(vmem_limit_bytes=40 << 20),
        cost_estimate=pl.CostEstimate(flops=20_000_000, bytes_accessed=3_000_000, transcendentals=0),
        name="fine",
    )(pos, m2, m1, own, p1, p2)


def speed_kernel(own_ref, speed_ref, ev):
    row = lax.broadcasted_iota(jnp.int32, (256, 128), 0)
    col = lax.broadcasted_iota(jnp.int32, (256, 128), 1)
    pool = (row // 2 == col).astype(F32)
    rows = own_ref[...].reshape(192, 256)
    ev[...] = jnp.dot(rows, pool, precision=HI, preferred_element_type=F32)
    x2 = ev[pl.ds(0, 96, stride=2), :] + ev[pl.ds(1, 96, stride=2), :]
    x2 = x2.reshape(3, 2, 2, 8, 128)
    speed_ref[...] = (x2[:, :, 0] + x2[:, :, 1]) * 0.25


def coarse_speed(own):
    vm = pl.BlockSpec(memory_space=VM)
    return pl.pallas_call(
        speed_kernel,
        out_shape=jax.ShapeDtypeStruct((3, 2, 8, 128), F32),
        in_specs=[vm],
        out_specs=vm,
        scratch_shapes=[pltpu.VMEM((192, 128), F32)],
        cost_estimate=pl.CostEstimate(flops=1_000_000, bytes_accessed=200_000, transcendentals=0),
        name="speed",
    )(own)


def build_coefs(speed_ref, coefs, layers):
    def one(j, carry):
        def at(i):
            keep = jnp.where(jnp.logical_and(i >= 0, i < layers), 1.0, 0.0).astype(F32)
            k = jnp.clip(i, 0, layers - 1)
            return [speed_ref[k // 2, c, k % 2] * keep for c in range(3)]
        here = at(j)

        def store(i, x):
            coefs[j, i] = x
        coarse_coefs(at(j - 1), here, at(j + 1), jnp.float32(1.0), store)
        return carry
    lax.fori_loop(0, layers, one, 0)


def psi_layer(coefs, src, j):
    return psi(lambda i: coefs[j, i],
               [src[j, c] for c in range(3)],
               [src[j + 1, c] for c in range(3)],
               [src[j + 2, c] for c in range(3)])


def finish(first, start_ref, relaxed_ref, coarse, out_ref, ev, od):
    for c in range(3):
        for zc in range(2):
            w = [[jnp.where(first, start_ref[c, 2 * zc + dz, k], relaxed_ref[c, 2 * zc + dz, k])
                  for k in range(4)] for dz in range(2)]
            lo, hi = [(v[0] + v[1]) + (v[2] + v[3]) for v in w]
            mean = (lo + hi) * 0.125
            diff = jnp.where(first, mean, coarse(c, zc)) - mean
            for dz in range(2):
                row0 = (c * 4 + 2 * zc + dz) * 16
                for q in range(2):
                    ev[pl.ds(row0 + q, 8, stride=2), :] = w[dz][2 * q] + diff
                    od[pl.ds(row0 + q, 8, stride=2), :] = w[dz][2 * q + 1] + diff
    both = jnp.concatenate([ev[...], od[...]], axis=1)
    out = jnp.dot(both, lane_parity(True), precision=HI, preferred_element_type=F32)
    out_ref[...] = out.reshape(3, 4, 16, 256)


def sweep_all_kernel(pos_ref, start_ref, relaxed_ref, coarse1_ref, speed_ref, g_hbm, out_ref,
                     coefs, state_a, state_b, keep, g_buf, ev, od, sems):
    slab, t = pos_ref[0], pos_ref[1]
    layers = 2 * speed_ref.shape[0]
    turns = g_hbm.shape[0] - 2

    def fetch(k, slot):
        return pltpu.make_async_copy(g_hbm.at[k], g_buf.at[slot], sems.at[slot])
    fetch(0, 0).start()
    build_coefs(speed_ref, coefs, layers)
    for ref in (state_a, state_b):
        ref[...] = jnp.zeros_like(ref)
    keep[...] = coarse1_ref[...]

    def step(k, src, dst, slot):
        fetch(k, slot).wait()

        @pl.when(k + 1 < turns)
        def _():
            fetch(k + 1, 1 - slot).start()

        def layer(j, carry):
            new = psi_layer(coefs, src, j)
            for c in range(3):
                dst[j + 1, c] = new[c] + g_buf[slot, j // 2, c, j % 2]
            return carry
        lax.fori_loop(0, layers, layer, 0)

        @pl.when(k + 2 == t)
        def _():
            for i in range(2):
                for c in range(3):
                    keep[c, i] = dst[1 + 2 * slab + i, c]

    def two(i, carry):
        step(2 * i, state_a, state_b, 0)
        step(2 * i + 1, state_b, state_a, 1)
        return carry
    lax.fori_loop(0, turns // 2, two, 0)
    finish(t == 0, start_ref, relaxed_ref, lambda c, zc: keep[c, zc], out_ref, ev, od)


def sweep_all(pos, start, relaxed, coarse1, speed, g):
    vm = pl.BlockSpec(memory_space=VM)
    layers = 2 * speed.shape[0]
    return pl.pallas_call(
        sweep_all_kernel,
        out_shape=jax.ShapeDtypeStruct((3, 4, 16, 256), F32),
        in_specs=[pl.BlockSpec(memory_space=pltpu.MemorySpace.SMEM)] + [vm] * 4 + [pl.BlockSpec(memory_space=pl.ANY)],
        out_specs=vm,
        scratch_shapes=[
            pltpu.VMEM((layers, 15, 8, 128), F32),
            pltpu.VMEM((layers + 2, 3, 8, 128), F32),
            pltpu.VMEM((layers + 2, 3, 8, 128), F32),
            pltpu.VMEM((3, 2, 8, 128), F32),
            pltpu.VMEM((2,) + g.shape[1:], F32),
            pltpu.VMEM((192, 128), F32),
            pltpu.VMEM((192, 128), F32),
            pltpu.SemaphoreType.DMA((2,)),
        ],
        compiler_params=pltpu.CompilerParams(vmem_limit_bytes=16 << 20),
        cost_estimate=pl.CostEstimate(flops=50_000_000, bytes_accessed=13_000_000, transcendentals=0),
        name="sweep",
    )(pos, start, relaxed, coarse1, speed, g)


def moved(block, by):
    count = lax.axis_size("gz")
    route = [(i, i + by) for i in range(count) if 0 <= i + by < count]
    return lax.ppermute(block, "gz", route)


def local(c_states, velocity):
    slab = lax.axis_index("gz")
    t = lax.axis_index("tm")
    intervals, slabs = lax.axis_size("tm"), lax.axis_size("gz")
    depth = slabs * velocity.shape[1]
    own = jnp.concatenate([c_states[0], velocity], axis=0)
    m2, m1, p1, p2 = [moved(own, by) for by in (2, 1, -1, -2)]
    speed = lax.all_gather(coarse_speed(velocity), "gz")
    pos = jnp.stack([slab, (t == 0).astype(jnp.int32), jnp.int32(depth)])
    start, after, forcing, coarse1 = fine(pos, m2, m1, own, p1, p2)
    route = [(i, i + 1) for i in range(intervals - 1)]
    relaxed = lax.ppermute(after, "tm", route)
    coarse1 = lax.ppermute(coarse1, "tm", route)
    forcing = lax.all_gather(forcing, ("tm", "gz"))
    forcing = forcing.reshape((intervals, slabs) + forcing.shape[1:])
    out = sweep_all(jnp.stack([slab, t]), start, relaxed, coarse1, speed, forcing)
    return out[None]


def solution(mesh):
    return jax.shard_map(
        local,
        mesh=mesh,
        in_specs=(P("tm", None, "gz", None, None), P(None, "gz", None, None)),
        out_specs=P("tm", None, "gz", None, None),
        check_vma=False,
    )
```

```python
import functools
import jax
import jax.numpy as jnp
from jax import lax
from jax.experimental import pallas as pl
from jax.experimental.pallas import tpu as pltpu
from jax.sharding import PartitionSpec as P

STEPS = 4
KAPPA = 0.04
FINE_UNROLL = 2
F32 = jnp.float32
HI = lax.Precision.HIGHEST
VM = pltpu.MemorySpace.VMEM


def lane_parity(transpose=False):
    row = lax.broadcasted_iota(jnp.int32, (256, 256), 1 if transpose else 0)
    col = lax.broadcasted_iota(jnp.int32, (256, 256), 0 if transpose else 1)
    want = 2 * (col % 128) + col // 128
    return (row == want).astype(F32)


def shift(v, by, axis, masked_at, index):
    return jnp.where(index == masked_at, 0.0, pltpu.roll(v, by % v.shape[axis], axis))


def stencil_terms(low, high, mid, inside):
    a = [KAPPA + jnp.maximum(mid[d], 0.0) for d in range(3)]
    b = [KAPPA - jnp.minimum(mid[d], 0.0) for d in range(3)]
    centre = 1.0 - (a[0] + b[0] + a[1] + b[1] + a[2] + b[2])
    m = [[(high[e][c] - low[e][c]) * 0.5 for e in range(3)] for c in range(3)]
    for c in range(3):
        m[c][c] = m[c][c] + centre
    a = [x * inside for x in a]
    b = [x * inside for x in b]
    m = [[x * inside for x in row] for row in m]
    return a, b, m


def iotas():
    sub = lax.broadcasted_iota(jnp.int32, (8, 128), 0)
    lane = lax.broadcasted_iota(jnp.int32, (8, 128), 1)
    return sub, lane


def coarse_coefs(below, here, above, inside, store):
    sub, lane = iotas()
    low = [below, [shift(v, 1, 0, 0, sub) for v in here], [shift(v, 1, 1, 0, lane) for v in here]]
    high = [above, [shift(v, -1, 0, 7, sub) for v in here], [shift(v, -1, 1, 127, lane) for v in here]]
    a, b, m = stencil_terms(low, high, here, inside)
    a[1] = jnp.where(sub == 0, 0.0, a[1])
    b[1] = jnp.where(sub == 7, 0.0, b[1])
    a[2] = jnp.where(lane == 0, 0.0, a[2])
    b[2] = jnp.where(lane == 127, 0.0, b[2])
    flat = a + b + m[0] + m[1] + m[2]
    for i, x in enumerate(flat):
        store(i, x)


def psi(coef, below, here, above):
    a = [coef(i) for i in range(3)]
    b = [coef(3 + i) for i in range(3)]
    out = []
    for c in range(3):
        w = here[c]
        acc = a[0] * below[c] + b[0] * above[c]
        acc = acc + (a[1] * pltpu.roll(w, 1, 0) + b[1] * pltpu.roll(w, 7, 0))
        acc = acc + (a[2] * pltpu.roll(w, 1, 1) + b[2] * pltpu.roll(w, 127, 1))
        acc = acc + (coef(6 + 3 * c) * here[0] + coef(7 + 3 * c) * here[1] + coef(8 + 3 * c) * here[2])
        out.append(acc)
    return out


NL = 12
VSPEC = pl.BlockSpec(memory_space=VM)
SSPEC = pl.BlockSpec(memory_space=pltpu.MemorySpace.SMEM)
GRANT = 40 << 20


def shaped(*dims):
    return jax.ShapeDtypeStruct(dims, F32)


def cost(flops, moved):
    return pl.CostEstimate(flops=flops, bytes_accessed=moved, transcendentals=0)


def march4(coefs, first, second, base):
    src, dst = first, second
    for k in range(1, STEPS + 1):
        def layer(l, carry, src=src, dst=dst):
            w = [[src[c, l, k] for k in range(4)] for c in range(3)]
            for q in range(2):
                for p in range(2):
                    k = 2 * q + p
                    kx = 2 * (1 - q) + p
                    ky = 2 * q + 1 - p
                    cf = [coefs[l, k, i] for i in range(15)]
                    for c in range(3):
                        xo = w[c][kx]
                        xr = pltpu.roll(xo, 7 if q else 1, 0)
                        yo = w[c][ky]
                        yr = pltpu.roll(yo, 127 if p else 1, 1)
                        acc = cf[0] * src[c, l - 1, k] + cf[3] * src[c, l + 1, k]
                        acc = acc + (cf[1] * (xo if q else xr) + cf[4] * (xr if q else xo))
                        acc = acc + (cf[2] * (yo if p else yr) + cf[5] * (yr if p else yo))
                        acc = acc + (cf[6 + 3 * c] * w[0][k] + cf[7 + 3 * c] * w[1][k] + cf[8 + 3 * c] * w[2][k])
                        dst[c, l, k] = acc
            return carry
        lax.fori_loop(k, NL - k, layer, 0, unroll=FINE_UNROLL)
        src, dst = dst, src


def restrict(src, j):
    out = []
    for c in range(3):
        lo = (src[c, 2 * j, 0] + src[c, 2 * j, 1]) + (src[c, 2 * j, 2] + src[c, 2 * j, 3])
        hi = (src[c, 2 * j + 1, 0] + src[c, 2 * j + 1, 1]) + (src[c, 2 * j + 1, 2] + src[c, 2 * j + 1, 3])
        out.append((lo + hi) * 0.125)
    return out


def fine1_kernel(pos_ref, m1_ref, own_ref, p1_ref, start_ref, after_ref, coefs, speed_c_ref,
                 state_a, state_b, speed, ev, od):
    slab = pos_ref[0]
    depth = pos_ref[2]
    perm = lane_parity()
    for i, ref in enumerate((m1_ref, own_ref, p1_ref)):
        rows = ref[...].reshape(384, 256)
        both = jnp.dot(rows, perm, precision=HI, preferred_element_type=F32)
        ev[...] = both[:, :128]
        od[...] = both[:, 128:]
        for part, dest in ((0, state_a), (1, speed)):
            for q in range(2):
                for p, half in ((0, ev), (1, od)):
                    got = half[pl.ds(192 * part + q, 96, stride=2), :]
                    dest[:, 4 * i:4 * i + 4, 2 * q + p] = got.reshape(3, 4, 8, 128)
    start_ref[...] = state_a[...]
    sub, lane = iotas()

    def build(l, carry):
        z = slab * 4 + l - 4
        inside = jnp.where(jnp.logical_and(z >= 0, z < depth), 1.0, 0.0).astype(F32)
        mid = [[speed[c, l, k] for c in range(3)] for k in range(4)]
        for q in range(2):
            for p in range(2):
                k = 2 * q + p
                here = mid[k]
                xo = mid[2 * (1 - q) + p]
                yo = mid[2 * q + 1 - p]
                low_z = [speed[c, l - 1, k] for c in range(3)]
                high_z = [speed[c, l + 1, k] for c in range(3)]
                low_x = xo if q else [shift(v, 1, 0, 0, sub) for v in xo]
                high_x = [shift(v, -1, 0, 7, sub) for v in xo] if q else xo
                low_y = yo if p else [shift(v, 1, 1, 0, lane) for v in yo]
                high_y = [shift(v, -1, 1, 127, lane) for v in yo] if p else yo
                a, b, m = stencil_terms([low_z, low_x, low_y], [high_z, high_x, high_y], here, inside)
                if q:
                    b[1] = jnp.where(sub == 7, 0.0, b[1])
                else:
                    a[1] = jnp.where(sub == 0, 0.0, a[1])
                if p:
                    b[2] = jnp.where(lane == 127, 0.0, b[2])
                else:
                    a[2] = jnp.where(lane == 0, 0.0, a[2])
                for i, x in enumerate(a + b + m[0] + m[1] + m[2]):
                    coefs[l, k, i] = x
        return carry

    lax.fori_loop(1, NL - 1, build, 0)
    for j in range(1, 5):
        for c, v in enumerate(restrict(speed, j)):
            speed_c_ref[j - 1, c] = 2.0 * v
    march4(coefs, state_a, state_b, 0)
    after_ref[...] = state_a[:, 4:8]


def fine1(pos, m1, own, p1):
    return pl.pallas_call(
        fine1_kernel,
        out_shape=(shaped(3, NL, 4, 8, 128), shaped(3, 4, 4, 8, 128), shaped(NL, 4, 15, 8, 128), shaped(4, 3, 8, 128)),
        in_specs=[SSPEC] + [VSPEC] * 3,
        out_specs=(VSPEC,) * 4,
        scratch_shapes=[pltpu.VMEM((3, NL, 4, 8, 128), F32)] * 3 + [pltpu.VMEM((384, 128), F32)] * 2,
        compiler_params=pltpu.CompilerParams(vmem_limit_bytes=GRANT),
        cost_estimate=cost(10_000_000, 6_000_000),
        name="fine1",
    )(pos, m1, own, p1)


def fine2_kernel(pos_ref, coefs, speed_c, start_ref, m1_ref, own_ref, p1_ref, relaxed_ref, share_ref, state_a, state_b):
    slab = pos_ref[0]
    first = pos_ref[1] == 1
    depth = pos_ref[2]
    for i, ref in enumerate((m1_ref, own_ref, p1_ref)):
        for dz in range(4):
            l = 4 * i + dz
            for c in range(3):
                for k in range(4):
                    state_a[c, l, k] = jnp.where(first, start_ref[c, l, k], ref[c, dz, k])
    relaxed_ref[...] = state_a[:, 4:8]
    coarse = {j: restrict(state_a, j) for j in range(1, 5)}
    image = {}
    for j in (2, 3):
        cc = {}
        coarse_coefs(*[[speed_c[i, c] for c in range(3)] for i in (j - 2, j - 1, j)], jnp.float32(1.0), cc.__setitem__)
        image[j] = psi(cc.__getitem__, coarse[j - 1], coarse[j], coarse[j + 1])
    march4(coefs, state_a, state_b, 0)
    for i, j in enumerate((2, 3)):
        again = restrict(state_a, j)
        for c in range(3):
            forcing = again[c] - image[j][c]
            forcing = forcing + jnp.where(first, image[j][c], 0.0)
            for s in range(share_ref.shape[0]):
                share_ref[s, 0, i, c] = forcing
                share_ref[s, 1, i, c] = speed_c[j - 1, c]


def fine2(pos, coefs, speed_c, start, m1, own, p1, slabs):
    return pl.pallas_call(
        fine2_kernel,
        out_shape=(shaped(3, 4, 4, 8, 128), shaped(slabs, 2, 2, 3, 8, 128)),
        in_specs=[SSPEC] + [VSPEC] * 6,
        out_specs=(VSPEC,) * 2,
        scratch_shapes=[pltpu.VMEM((3, NL, 4, 8, 128), F32)] * 2,
        compiler_params=pltpu.CompilerParams(vmem_limit_bytes=GRANT),
        cost_estimate=cost(10_000_000, 6_000_000),
        name="fine2",
    )(pos, coefs, speed_c, start, m1, own, p1)


def coefs_kernel(speed_ref, coefs):
    layers = speed_ref.shape[0]

    def one(j, carry):
        def at(i):
            keep = jnp.where(jnp.logical_and(i >= 0, i < layers), 1.0, 0.0).astype(F32)
            k = jnp.clip(i, 0, layers - 1)
            return [speed_ref[k, c] * keep for c in range(3)]

        def store(i, x):
            coefs[j, i] = x
        coarse_coefs(at(j - 1), at(j), at(j + 1), jnp.float32(1.0), store)
        return carry
    lax.fori_loop(0, layers, one, 0, unroll=2)


def sweep_coefs(speed):
    return pl.pallas_call(
        coefs_kernel,
        out_shape=shaped(speed.shape[0], 15, 8, 128),
        in_specs=[VSPEC],
        out_specs=VSPEC,
        compiler_params=pltpu.CompilerParams(vmem_limit_bytes=GRANT),
        cost_estimate=cost(3_000_000, 2_400_000),
        name="coefs",
    )(speed)


CHUNK = 4


def window(slab, halo, layers):
    count = min(layers, 2 + 2 * halo)
    return count, jnp.clip(2 * slab - halo, 0, layers - count)


def psi_steps(coefs, src, dst, slab, halo, steps):
    layers = coefs.shape[0]
    for s in range(steps):
        reach = halo + steps - 1 - s
        low = jnp.maximum(2 * slab - reach, 0) // CHUNK
        high = (jnp.minimum(2 * slab + 2 + reach, layers) + CHUNK - 1) // CHUNK
        src, dst = psi_step(coefs, src, dst, low, high)
    return src


def psi_step(coefs, src, dst, low, high):
    def some(i, carry):
        for dj in range(CHUNK):
            j = i * CHUNK + dj
            new = psi(lambda n: coefs[j, n],
                      [src[j, c] for c in range(3)],
                      [src[j + 1, c] for c in range(3)],
                      [src[j + 2, c] for c in range(3)])
            for c in range(3):
                dst[j + 1, c] = new[c]
        return carry
    lax.fori_loop(low, high, some, 0)
    return dst, src


def round_kernel(distance, halo_own, halo_out, pos_ref, coefs, own_ref, got_ref, out_ref, state_a, state_b):
    slab = pos_ref[0]
    layers = coefs.shape[0]
    n_got, at_got = window(slab, halo_out + distance, layers)
    n_own, at_own = window(slab, halo_own, layers)
    n_out, at_out = window(slab, halo_out, layers)
    for ref in (state_a, state_b):
        ref[0] = jnp.zeros((3, 8, 128), F32)
        ref[layers + 1] = jnp.zeros((3, 8, 128), F32)
    state_a[pl.ds(at_got + 1, n_got)] = got_ref[...]
    if distance >= 4:
        def pair(i, carry):
            reach = halo_out + distance - 1 - 2 * i

            def span(r):
                low = jnp.maximum(2 * slab - r, 0) // CHUNK
                return low, (jnp.minimum(2 * slab + 2 + r, layers) + CHUNK - 1) // CHUNK
            psi_step(coefs, state_a, state_b, *span(reach))
            psi_step(coefs, state_b, state_a, *span(reach - 1))
            return carry
        lax.fori_loop(0, distance // 2, pair, 0)
        last = state_a
    else:
        last = psi_steps(coefs, state_a, state_b, slab, halo_out, distance)
    out_ref[...] = last[pl.ds(at_out + 1, n_out)] + own_ref[pl.ds(at_out - at_own, n_out)]


def sweep_round(distance, halo_own, halo_out, pos, coefs, own, got):
    layers = coefs.shape[0]
    count = min(layers, 2 + 2 * halo_out)
    return pl.pallas_call(
        functools.partial(round_kernel, distance, halo_own, halo_out),
        out_shape=shaped(count, 3, 8, 128),
        in_specs=[SSPEC] + [VSPEC] * 3,
        out_specs=VSPEC,
        scratch_shapes=[pltpu.VMEM((layers + 2, 3, 8, 128), F32)] * 2,
        compiler_params=pltpu.CompilerParams(vmem_limit_bytes=GRANT),
        cost_estimate=cost(distance * 2_000_000, 3_000_000),
        name=f"round{distance}",
    )(pos, coefs, own, got)


def last_kernel(pos_ref, coefs, relaxed_ref, near_ref, far_ref, out_ref, state_a, ev, od):
    slab = pos_ref[0]
    first = pos_ref[1] == 1
    layers = coefs.shape[0]
    n_got, at_got = window(slab, 1, layers)
    state_a[0] = jnp.zeros((3, 8, 128), F32)
    state_a[layers + 1] = jnp.zeros((3, 8, 128), F32)
    state_a[pl.ds(at_got + 1, n_got)] = far_ref[...]
    for zc in range(2):
        j = 2 * slab + zc
        new = psi(lambda n: coefs[j, n], *[[state_a[j + d, c] for c in range(3)] for d in range(3)])
        for c in range(3):
            coarse = new[c] + near_ref[j - at_got, c]
            w = [[relaxed_ref[c, 2 * zc + dz, k] for k in range(4)] for dz in range(2)]
            lo, hi = [(v[0] + v[1]) + (v[2] + v[3]) for v in w]
            mean = (lo + hi) * 0.125
            diff = jnp.where(first, mean, coarse) - mean
            for dz in range(2):
                row0 = (c * 4 + 2 * zc + dz) * 16
                for q in range(2):
                    ev[pl.ds(row0 + q, 8, stride=2), :] = w[dz][2 * q] + diff
                    od[pl.ds(row0 + q, 8, stride=2), :] = w[dz][2 * q + 1] + diff
    both = jnp.concatenate([ev[...], od[...]], axis=1)
    out = jnp.dot(both, lane_parity(True), precision=HI, preferred_element_type=F32)
    out_ref[...] = out.reshape(3, 4, 16, 256)


def sweep_last(pos, coefs, relaxed, near, far):
    layers = coefs.shape[0]
    return pl.pallas_call(
        last_kernel,
        out_shape=shaped(3, 4, 16, 256),
        in_specs=[SSPEC] + [VSPEC] * 4,
        out_specs=VSPEC,
        scratch_shapes=[pltpu.VMEM((layers + 2, 3, 8, 128), F32)] + [pltpu.VMEM((192, 128), F32)] * 2,
        compiler_params=pltpu.CompilerParams(vmem_limit_bytes=GRANT),
        cost_estimate=cost(2_000_000, 3_000_000),
        name="last",
    )(pos, coefs, relaxed, near, far)


def moved(block, by_t, by_z):
    nt, nz = lax.axis_size("tm"), lax.axis_size("gz")
    route = [
        ((t - by_t) * nz + z - by_z, t * nz + z)
        for t in range(nt) for z in range(nz)
        if 0 <= t - by_t < nt and 0 <= z - by_z < nz
    ]
    return lax.ppermute(block, ("tm", "gz"), route)


def local(c_states, velocity):
    slab = lax.axis_index("gz")
    t = lax.axis_index("tm")
    slabs = lax.axis_size("gz")
    depth = slabs * velocity.shape[1]
    pos = jnp.stack([slab, (t == 0).astype(jnp.int32), jnp.int32(depth)])
    own = jnp.concatenate([c_states[0], velocity], axis=0)
    start, after, coefs, speed_c = fine1(pos, moved(own, 0, 1), own, moved(own, 0, -1))
    m1, same, p1 = [moved(after, 1, by) for by in (1, 0, -1)]
    relaxed, share = fine2(pos, coefs, speed_c, start, m1, same, p1, slabs)
    share = lax.all_to_all(share, "gz", 0, 0, tiled=True)
    state = share[:, 0].reshape(2 * slabs, 3, 8, 128)
    coefs = sweep_coefs(share[:, 1].reshape(2 * slabs, 3, 8, 128))
    halo_own = slabs * 2
    for distance in (16, 8, 4, 2):
        state = sweep_round(distance, halo_own, distance - 1, pos, coefs, state, moved(state, distance, 0))
        halo_own = distance - 1
    out = sweep_last(pos, coefs, relaxed, moved(state, 1, 0), moved(state, 2, 0))
    return out[None]


def solution(mesh):
    return jax.shard_map(
        local,
        mesh=mesh,
        in_specs=(P("tm", None, "gz", None, None), P(None, "gz", None, None)),
        out_specs=P("tm", None, "gz", None, None),
        check_vma=False,
    )
```

```python
import functools
import jax
import jax.numpy as jnp
from jax import lax
from jax.experimental import pallas as pl
from jax.experimental.pallas import tpu as pltpu
from jax.sharding import PartitionSpec as P

STEPS = 4
KAPPA = 0.04
FINE_UNROLL = 2
FULL_CHUNK = 8
F32 = jnp.float32
HI = lax.Precision.HIGHEST
VM = pltpu.MemorySpace.VMEM


def lane_parity(transpose=False):
    row = lax.broadcasted_iota(jnp.int32, (256, 256), 1 if transpose else 0)
    col = lax.broadcasted_iota(jnp.int32, (256, 256), 0 if transpose else 1)
    want = 2 * (col % 128) + col // 128
    return (row == want).astype(F32)


def shift(v, by, axis, masked_at, index):
    return jnp.where(index == masked_at, 0.0, pltpu.roll(v, by % v.shape[axis], axis))


def stencil_terms(low, high, mid, inside):
    a = [KAPPA + jnp.maximum(mid[d], 0.0) for d in range(3)]
    b = [KAPPA - jnp.minimum(mid[d], 0.0) for d in range(3)]
    centre = 1.0 - (a[0] + b[0] + a[1] + b[1] + a[2] + b[2])
    m = [[(high[e][c] - low[e][c]) * 0.5 for e in range(3)] for c in range(3)]
    for c in range(3):
        m[c][c] = m[c][c] + centre
    a = [x * inside for x in a]
    b = [x * inside for x in b]
    m = [[x * inside for x in row] for row in m]
    return a, b, m


def iotas():
    sub = lax.broadcasted_iota(jnp.int32, (8, 128), 0)
    lane = lax.broadcasted_iota(jnp.int32, (8, 128), 1)
    return sub, lane


def coarse_coefs(below, here, above, inside, store):
    sub, lane = iotas()
    low = [below, [shift(v, 1, 0, 0, sub) for v in here], [shift(v, 1, 1, 0, lane) for v in here]]
    high = [above, [shift(v, -1, 0, 7, sub) for v in here], [shift(v, -1, 1, 127, lane) for v in here]]
    a, b, m = stencil_terms(low, high, here, inside)
    a[1] = jnp.where(sub == 0, 0.0, a[1])
    b[1] = jnp.where(sub == 7, 0.0, b[1])
    a[2] = jnp.where(lane == 0, 0.0, a[2])
    b[2] = jnp.where(lane == 127, 0.0, b[2])
    flat = a + b + m[0] + m[1] + m[2]
    for i, x in enumerate(flat):
        store(i, x)


def psi(coef, below, here, above):
    a = [coef(i) for i in range(3)]
    b = [coef(3 + i) for i in range(3)]
    out = []
    for c in range(3):
        w = here[c]
        acc = a[0] * below[c] + b[0] * above[c]
        acc = acc + (a[1] * pltpu.roll(w, 1, 0) + b[1] * pltpu.roll(w, 7, 0))
        acc = acc + (a[2] * pltpu.roll(w, 1, 1) + b[2] * pltpu.roll(w, 127, 1))
        acc = acc + (coef(6 + 3 * c) * here[0] + coef(7 + 3 * c) * here[1] + coef(8 + 3 * c) * here[2])
        out.append(acc)
    return out


NL = 12
VSPEC = pl.BlockSpec(memory_space=VM)
HSPEC = pl.BlockSpec(memory_space=pltpu.MemorySpace.HBM)
SSPEC = pl.BlockSpec(memory_space=pltpu.MemorySpace.SMEM)
GRANT = 16 << 20


def shaped(*dims):
    return jax.ShapeDtypeStruct(dims, F32)


def cost(flops, moved):
    return pl.CostEstimate(flops=flops, bytes_accessed=moved, transcendentals=0)


def march4(coefs, first, second, base):
    src, dst = first, second
    for k in range(1, STEPS + 1):
        def layer(l, carry, src=src, dst=dst):
            w = [[src[c, l, k] for k in range(4)] for c in range(3)]
            for q in range(2):
                for p in range(2):
                    k = 2 * q + p
                    kx = 2 * (1 - q) + p
                    ky = 2 * q + 1 - p
                    cf = [coefs[l, k, i] for i in range(15)]
                    for c in range(3):
                        xo = w[c][kx]
                        xr = pltpu.roll(xo, 7 if q else 1, 0)
                        yo = w[c][ky]
                        yr = pltpu.roll(yo, 127 if p else 1, 1)
                        acc = cf[0] * src[c, l - 1, k] + cf[3] * src[c, l + 1, k]
                        acc = acc + (cf[1] * (xo if q else xr) + cf[4] * (xr if q else xo))
                        acc = acc + (cf[2] * (yo if p else yr) + cf[5] * (yr if p else yo))
                        acc = acc + (cf[6 + 3 * c] * w[0][k] + cf[7 + 3 * c] * w[1][k] + cf[8 + 3 * c] * w[2][k])
                        dst[c, l, k] = acc
            return carry
        lax.fori_loop(k, NL - k, layer, 0, unroll=FINE_UNROLL)
        src, dst = dst, src


def restrict(src, j):
    out = []
    for c in range(3):
        lo = (src[c, 2 * j, 0] + src[c, 2 * j, 1]) + (src[c, 2 * j, 2] + src[c, 2 * j, 3])
        hi = (src[c, 2 * j + 1, 0] + src[c, 2 * j + 1, 1]) + (src[c, 2 * j + 1, 2] + src[c, 2 * j + 1, 3])
        out.append((lo + hi) * 0.125)
    return out


def fine1_kernel(pos_ref, m1_ref, own_ref, p1_ref, start_ref, after_ref, coefs, speed_c_ref, share_ref,
                 state_a, state_b, begin, speed, share, ev, od, sems):
    slab = pos_ref[0]
    depth = pos_ref[2]
    perm = lane_parity()
    for i, ref in enumerate((m1_ref, own_ref, p1_ref)):
        rows = ref[...].reshape(384, 256)
        both = jnp.dot(rows, perm, precision=HI, preferred_element_type=F32)
        ev[...] = both[:, :128]
        od[...] = both[:, 128:]
        for part, dest in ((0, state_a), (1, speed)):
            for q in range(2):
                for p, half in ((0, ev), (1, od)):
                    got = half[pl.ds(192 * part + q, 96, stride=2), :]
                    dest[:, 4 * i:4 * i + 4, 2 * q + p] = got.reshape(3, 4, 8, 128)
    begin[...] = state_a[...]
    keep = pltpu.make_async_copy(begin, start_ref, sems.at[0])
    keep.start()
    sub, lane = iotas()

    def build(l, carry):
        z = slab * 4 + l - 4
        inside = jnp.where(jnp.logical_and(z >= 0, z < depth), 1.0, 0.0).astype(F32)
        mid = [[speed[c, l, k] for c in range(3)] for k in range(4)]
        for q in range(2):
            for p in range(2):
                k = 2 * q + p
                here = mid[k]
                xo = mid[2 * (1 - q) + p]
                yo = mid[2 * q + 1 - p]
                low_z = [speed[c, l - 1, k] for c in range(3)]
                high_z = [speed[c, l + 1, k] for c in range(3)]
                low_x = xo if q else [shift(v, 1, 0, 0, sub) for v in xo]
                high_x = [shift(v, -1, 0, 7, sub) for v in xo] if q else xo
                low_y = yo if p else [shift(v, 1, 1, 0, lane) for v in yo]
                high_y = [shift(v, -1, 1, 127, lane) for v in yo] if p else yo
                a, b, m = stencil_terms([low_z, low_x, low_y], [high_z, high_x, high_y], here, inside)
                if q:
                    b[1] = jnp.where(sub == 7, 0.0, b[1])
                else:
                    a[1] = jnp.where(sub == 0, 0.0, a[1])
                if p:
                    b[2] = jnp.where(lane == 127, 0.0, b[2])
                else:
                    a[2] = jnp.where(lane == 0, 0.0, a[2])
                for i, x in enumerate(a + b + m[0] + m[1] + m[2]):
                    coefs[l, k, i] = x
        return carry

    lax.fori_loop(1, NL - 1, build, 0)
    for j in range(1, 5):
        for c, v in enumerate(restrict(speed, j)):
            speed_c_ref[j - 1, c] = 2.0 * v
            if j in (2, 3):
                for to in range(share.shape[0]):
                    share[to, j - 2, c] = 2.0 * v
    send = pltpu.make_async_copy(share, share_ref, sems.at[1])
    send.start()
    march4(coefs, state_a, state_b, 0)
    after_ref[...] = state_a[:, 4:8]
    keep.wait()
    send.wait()


def fine1(pos, m1, own, p1, slabs):
    return pl.pallas_call(
        fine1_kernel,
        out_shape=(shaped(3, NL, 4, 8, 128), shaped(3, 4, 4, 8, 128), shaped(NL, 4, 15, 8, 128),
                   shaped(4, 3, 8, 128), shaped(slabs, 2, 3, 8, 128)),
        in_specs=[SSPEC] + [VSPEC] * 3,
        out_specs=(HSPEC, VSPEC, VSPEC, VSPEC, HSPEC),
        scratch_shapes=[pltpu.VMEM((3, NL, 4, 8, 128), F32)] * 4 + [pltpu.VMEM((slabs, 2, 3, 8, 128), F32)]
        + [pltpu.VMEM((384, 128), F32)] * 2 + [pltpu.SemaphoreType.DMA((2,))],
        compiler_params=pltpu.CompilerParams(vmem_limit_bytes=GRANT),
        cost_estimate=cost(10_000_000, 6_000_000),
        name="fine1",
    )(pos, m1, own, p1)


def fine2_kernel(pos_ref, coefs, speed_c, start_ref, m1_ref, own_ref, p1_ref, relaxed_ref, forcing_ref, state_a, state_b, sem):
    slab = pos_ref[0]
    first = pos_ref[1] == 1
    depth = pos_ref[2]
    @pl.when(first)
    def _():
        fetch = pltpu.make_async_copy(start_ref, state_a, sem)
        fetch.start()
        fetch.wait()

    @pl.when(jnp.logical_not(first))
    def _():
        for i, ref in enumerate((m1_ref, own_ref, p1_ref)):
            state_a[:, 4 * i:4 * i + 4] = ref[...]
    relaxed_ref[...] = state_a[:, 4:8]
    coarse = {j: restrict(state_a, j) for j in range(1, 5)}
    image = {}
    for j in (2, 3):
        cc = {}
        coarse_coefs(*[[speed_c[i, c] for c in range(3)] for i in (j - 2, j - 1, j)], jnp.float32(1.0), cc.__setitem__)
        image[j] = psi(cc.__getitem__, coarse[j - 1], coarse[j], coarse[j + 1])
    march4(coefs, state_a, state_b, 0)
    for i, j in enumerate((2, 3)):
        again = restrict(state_a, j)
        for c in range(3):
            forcing = again[c] - image[j][c]
            forcing = forcing + jnp.where(first, image[j][c], 0.0)
            forcing_ref[i, c] = forcing


def fine2(pos, coefs, speed_c, start, m1, own, p1):
    return pl.pallas_call(
        fine2_kernel,
        out_shape=(shaped(3, 4, 4, 8, 128), shaped(2, 3, 8, 128)),
        in_specs=[SSPEC, VSPEC, VSPEC, HSPEC] + [VSPEC] * 3,
        out_specs=(VSPEC,) * 2,
        scratch_shapes=[pltpu.VMEM((3, NL, 4, 8, 128), F32)] * 2 + [pltpu.SemaphoreType.DMA],
        compiler_params=pltpu.CompilerParams(vmem_limit_bytes=GRANT),
        cost_estimate=cost(10_000_000, 6_000_000),
        name="fine2",
    )(pos, coefs, speed_c, start, m1, own, p1)


def coefs_kernel(speed_ref, coefs):
    layers = speed_ref.shape[0]

    def one(j, carry):
        def at(i):
            keep = jnp.where(jnp.logical_and(i >= 0, i < layers), 1.0, 0.0).astype(F32)
            k = jnp.clip(i, 0, layers - 1)
            return [speed_ref[k, c] * keep for c in range(3)]

        def store(i, x):
            coefs[j, i] = x
        coarse_coefs(at(j - 1), at(j), at(j + 1), jnp.float32(1.0), store)
        return carry
    lax.fori_loop(0, layers, one, 0, unroll=2)


def sweep_coefs(speed):
    return pl.pallas_call(
        coefs_kernel,
        out_shape=shaped(speed.shape[0], 15, 8, 128),
        in_specs=[VSPEC],
        out_specs=VSPEC,
        compiler_params=pltpu.CompilerParams(vmem_limit_bytes=GRANT),
        cost_estimate=cost(3_000_000, 2_400_000),
        name="coefs",
    )(speed)


def window(slab, halo, layers):
    count = min(layers, 2 + 2 * halo)
    return count, jnp.clip(2 * slab - halo, 0, layers - count)


def psi_step(coefs, src, dst, chunk, low, high):
    def some(i, carry):
        for dj in range(chunk):
            j = i * chunk + dj
            new = psi(lambda n: coefs[j, n],
                      [src[j, c] for c in range(3)],
                      [src[j + 1, c] for c in range(3)],
                      [src[j + 2, c] for c in range(3)])
            for c in range(3):
                dst[j + 1, c] = new[c]
        return carry
    lax.fori_loop(low, high, some, 0)


def spread(distance, halo, slab, coefs, got_ref, state_a, state_b):
    layers = coefs.shape[0]
    for ref in (state_a, state_b):
        ref[...] = jnp.zeros_like(ref)
    n_in, at_in = window(slab, halo, layers)
    state_a[pl.ds(at_in + 1, n_in)] = got_ref[...]
    src, dst = state_a, state_b
    chunk = 2 if distance == 1 else 4
    for s in range(distance):
        reach = halo + 1 + s
        low = jnp.maximum(2 * slab - reach, 0) // chunk
        high = (jnp.minimum(2 * slab + 2 + reach, layers) + chunk - 1) // chunk
        psi_step(coefs, src, dst, chunk, low, high)
        src, dst = dst, src
    return src, dst


def round_kernel(distance, halo, pos_ref, coefs, own_ref, got_ref, out_ref, state_a, state_b):
    slab = pos_ref[0]
    layers = coefs.shape[0]
    n_in, at_in = window(slab, halo, layers)
    n_out, at_out = window(slab, halo + distance, layers)
    last, _ = spread(distance, halo, slab, coefs, got_ref, state_a, state_b)
    out_ref[...] = last[pl.ds(at_out + 1, n_out)]
    inner = pl.ds(at_in - at_out, n_in)
    out_ref[inner] = out_ref[inner] + own_ref[...]


def final_kernel(distance, halo, pos_ref, coefs, own_ref, got_ref, share_ref, state_a, state_b):
    slab = pos_ref[0]
    layers = coefs.shape[0]
    n_in, at_in = window(slab, halo, layers)
    last, other = spread(distance, halo, slab, coefs, got_ref, state_a, state_b)
    inner = pl.ds(at_in + 1, n_in)
    last[inner] = last[inner] + own_ref[...]
    share_ref[:, 0] = last[1:layers + 1].reshape(layers // 2, 2, 3, 8, 128)

    def pair(i, carry):
        psi_step(coefs, last, other, FULL_CHUNK, 0, layers // FULL_CHUNK)
        psi_step(coefs, other, last, FULL_CHUNK, 0, layers // FULL_CHUNK)
        return carry
    lax.fori_loop(0, distance, pair, 0)
    share_ref[:, 1] = last[1:layers + 1].reshape(layers // 2, 2, 3, 8, 128)


def sweep_round(distance, halo, final, pos, coefs, own, got):
    layers = coefs.shape[0]
    out = shaped(layers // 2, 2, 2, 3, 8, 128) if final else shaped(min(layers, 2 + 2 * (halo + distance)), 3, 8, 128)
    return pl.pallas_call(
        functools.partial(final_kernel if final else round_kernel, distance, halo),
        out_shape=out,
        in_specs=[SSPEC] + [VSPEC] * 3,
        out_specs=VSPEC,
        scratch_shapes=[pltpu.VMEM((layers + 2, 3, 8, 128), F32)] * 2,
        compiler_params=pltpu.CompilerParams(vmem_limit_bytes=GRANT),
        cost_estimate=cost((3 if final else 1) * distance * 2_000_000, 3_000_000),
        name=f"round{distance}",
    )(pos, coefs, own, got)


def total_kernel(got_ref, near_ref, far_ref):
    for i in range(2):
        for c in range(3):
            for part, ref in ((0, near_ref), (1, far_ref)):
                terms = [got_ref[s, part, i, c] for s in range(got_ref.shape[0])]
                while len(terms) > 1:
                    terms = [a + b for a, b in zip(terms[::2], terms[1::2])] + terms[len(terms) // 2 * 2:]
                ref[i, c] = terms[0]


def totals(got):
    return pl.pallas_call(
        total_kernel,
        out_shape=(shaped(2, 3, 8, 128),) * 2,
        in_specs=[VSPEC],
        out_specs=(VSPEC,) * 2,
        compiler_params=pltpu.CompilerParams(vmem_limit_bytes=GRANT),
        cost_estimate=cost(200_000, 850_000),
        name="totals",
    )(got)


def last_kernel(pos_ref, relaxed_ref, near_ref, far_ref, out_ref, ev, od):
    first = pos_ref[1] == 1
    for zc in range(2):
        for c in range(3):
            w = [[relaxed_ref[c, 2 * zc + dz, k] for k in range(4)] for dz in range(2)]
            lo, hi = [(v[0] + v[1]) + (v[2] + v[3]) for v in w]
            mean = (lo + hi) * 0.125
            diff = jnp.where(first, mean, near_ref[zc, c] + far_ref[zc, c]) - mean
            for dz in range(2):
                row0 = (c * 4 + 2 * zc + dz) * 16
                for q in range(2):
                    ev[pl.ds(row0 + q, 8, stride=2), :] = w[dz][2 * q] + diff
                    od[pl.ds(row0 + q, 8, stride=2), :] = w[dz][2 * q + 1] + diff
    both = jnp.concatenate([ev[...], od[...]], axis=1)
    out = jnp.dot(both, lane_parity(True), precision=HI, preferred_element_type=F32)
    out_ref[...] = out.reshape(3, 4, 16, 256)


def sweep_last(pos, relaxed, near, far):
    return pl.pallas_call(
        last_kernel,
        out_shape=shaped(3, 4, 16, 256),
        in_specs=[SSPEC] + [VSPEC] * 3,
        out_specs=VSPEC,
        scratch_shapes=[pltpu.VMEM((192, 128), F32)] * 2,
        compiler_params=pltpu.CompilerParams(vmem_limit_bytes=GRANT),
        cost_estimate=cost(2_000_000, 500_000),
        name="last",
    )(pos, relaxed, near, far)


def moved(block, by_t, by_z):
    nt, nz = lax.axis_size("tm"), lax.axis_size("gz")
    route = [
        ((t - by_t) * nz + z - by_z, t * nz + z)
        for t in range(nt) for z in range(nz)
        if 0 <= t - by_t < nt and 0 <= z - by_z < nz
    ]
    return lax.ppermute(block, ("tm", "gz"), route)


def local(c_states, velocity):
    slab = lax.axis_index("gz")
    t = lax.axis_index("tm")
    slabs = lax.axis_size("gz")
    depth = slabs * velocity.shape[1]
    pos = jnp.stack([slab, (t == 0).astype(jnp.int32), jnp.int32(depth)])
    own = jnp.concatenate([c_states[0], velocity], axis=0)
    start, after, coefs, speed_c, share = fine1(pos, moved(own, 0, 1), own, moved(own, 0, -1), slabs)
    m1, same, p1 = [moved(after, 1, by) for by in (1, 0, -1)]
    speed = lax.all_to_all(share, "gz", 0, 0, tiled=True)
    relaxed, state = fine2(pos, coefs, speed_c, start, m1, same, p1)
    coefs = sweep_coefs(speed.reshape(2 * slabs, 3, 8, 128))
    for distance in (1, 2, 4, 8):
        state = sweep_round(distance, distance - 1, distance == 8, pos, coefs, state, moved(state, distance, 0))
    near, far = totals(lax.all_to_all(state, "gz", 0, 0, tiled=True))
    out = sweep_last(pos, relaxed, moved(near, 1, 0), moved(far, 17, 0))
    return out[None]


def solution(mesh):
    return jax.shard_map(
        local,
        mesh=mesh,
        in_specs=(P("tm", None, "gz", None, None), P(None, "gz", None, None)),
        out_specs=P("tm", None, "gz", None, None),
        check_vma=False,
    )
```

```python
import functools
import jax
import jax.numpy as jnp
from jax import lax
from jax.experimental import pallas as pl
from jax.experimental.pallas import tpu as pltpu
from jax.sharding import PartitionSpec as P


STEPS = 4
KAPPA = 0.04
FINE_UNROLL = 2
FULL_CHUNK = 8
F32 = jnp.float32
HI = lax.Precision.HIGHEST
VM = pltpu.MemorySpace.VMEM


def lane_parity(transpose=False):
    row = lax.broadcasted_iota(jnp.int32, (256, 256), 1 if transpose else 0)
    col = lax.broadcasted_iota(jnp.int32, (256, 256), 0 if transpose else 1)
    want = 2 * (col % 128) + col // 128
    return (row == want).astype(F32)


def shift(v, by, axis, masked_at, index):
    return jnp.where(index == masked_at, 0.0, pltpu.roll(v, by % v.shape[axis], axis))


def stencil_terms(low, high, mid, inside):
    a = [KAPPA + jnp.maximum(mid[d], 0.0) for d in range(3)]
    b = [KAPPA - jnp.minimum(mid[d], 0.0) for d in range(3)]
    centre = 1.0 - (a[0] + b[0] + a[1] + b[1] + a[2] + b[2])
    m = [[(high[e][c] - low[e][c]) * 0.5 for e in range(3)] for c in range(3)]
    for c in range(3):
        m[c][c] = m[c][c] + centre
    a = [x * inside for x in a]
    b = [x * inside for x in b]
    m = [[x * inside for x in row] for row in m]
    return a, b, m


def iotas():
    sub = lax.broadcasted_iota(jnp.int32, (8, 128), 0)
    lane = lax.broadcasted_iota(jnp.int32, (8, 128), 1)
    return sub, lane


def coarse_coefs(below, here, above, inside, store):
    sub, lane = iotas()
    low = [below, [shift(v, 1, 0, 0, sub) for v in here], [shift(v, 1, 1, 0, lane) for v in here]]
    high = [above, [shift(v, -1, 0, 7, sub) for v in here], [shift(v, -1, 1, 127, lane) for v in here]]
    a, b, m = stencil_terms(low, high, here, inside)
    a[1] = jnp.where(sub == 0, 0.0, a[1])
    b[1] = jnp.where(sub == 7, 0.0, b[1])
    a[2] = jnp.where(lane == 0, 0.0, a[2])
    b[2] = jnp.where(lane == 127, 0.0, b[2])
    flat = a + b + m[0] + m[1] + m[2]
    for i, x in enumerate(flat):
        store(i, x)


def psi(coef, below, here, above):
    a = [coef(i) for i in range(3)]
    b = [coef(3 + i) for i in range(3)]
    out = []
    for c in range(3):
        w = here[c]
        acc = a[0] * below[c] + b[0] * above[c]
        acc = acc + (a[1] * pltpu.roll(w, 1, 0) + b[1] * pltpu.roll(w, 7, 0))
        acc = acc + (a[2] * pltpu.roll(w, 1, 1) + b[2] * pltpu.roll(w, 127, 1))
        acc = acc + (coef(6 + 3 * c) * here[0] + coef(7 + 3 * c) * here[1] + coef(8 + 3 * c) * here[2])
        out.append(acc)
    return out


NL = 12
VSPEC = pl.BlockSpec(memory_space=VM)
HSPEC = pl.BlockSpec(memory_space=pltpu.MemorySpace.HBM)
SSPEC = pl.BlockSpec(memory_space=pltpu.MemorySpace.SMEM)
GRANT = 16 << 20


def shaped(*dims):
    return jax.ShapeDtypeStruct(dims, F32)


def cost(flops, moved):
    return pl.CostEstimate(flops=flops, bytes_accessed=moved, transcendentals=0)


def march4(coefs, first, second):
    src, dst = first, second
    for k in range(1, STEPS + 1):
        def layer(l, carry, src=src, dst=dst):
            w = [[src[c, l, k] for k in range(4)] for c in range(3)]
            for q in range(2):
                for p in range(2):
                    k = 2 * q + p
                    kx = 2 * (1 - q) + p
                    ky = 2 * q + 1 - p
                    cf = [coefs[l, k, i] for i in range(15)]
                    for c in range(3):
                        xo = w[c][kx]
                        xr = pltpu.roll(xo, 7 if q else 1, 0)
                        yo = w[c][ky]
                        yr = pltpu.roll(yo, 127 if p else 1, 1)
                        acc = cf[0] * src[c, l - 1, k] + cf[3] * src[c, l + 1, k]
                        acc = acc + (cf[1] * (xo if q else xr) + cf[4] * (xr if q else xo))
                        acc = acc + (cf[2] * (yo if p else yr) + cf[5] * (yr if p else yo))
                        acc = acc + (cf[6 + 3 * c] * w[0][k] + cf[7 + 3 * c] * w[1][k] + cf[8 + 3 * c] * w[2][k])
                        dst[c, l, k] = acc
            return carry
        lax.fori_loop(k, NL - k, layer, 0, unroll=FINE_UNROLL)
        src, dst = dst, src


def restrict(src, j):
    out = []
    for c in range(3):
        lo = (src[c, 2 * j, 0] + src[c, 2 * j, 1]) + (src[c, 2 * j, 2] + src[c, 2 * j, 3])
        hi = (src[c, 2 * j + 1, 0] + src[c, 2 * j + 1, 1]) + (src[c, 2 * j + 1, 2] + src[c, 2 * j + 1, 3])
        out.append((lo + hi) * 0.125)
    return out


def fine_coefs(slab, depth, speed, coefs):
    sub, lane = iotas()

    def build(l, carry):
        z = slab * 4 + l - 4
        inside = jnp.where(jnp.logical_and(z >= 0, z < depth), 1.0, 0.0).astype(F32)
        mid = [[speed[c, l, k] for c in range(3)] for k in range(4)]
        for q in range(2):
            for p in range(2):
                k = 2 * q + p
                here = mid[k]
                xo = mid[2 * (1 - q) + p]
                yo = mid[2 * q + 1 - p]
                low_z = [speed[c, l - 1, k] for c in range(3)]
                high_z = [speed[c, l + 1, k] for c in range(3)]
                low_x = xo if q else [shift(v, 1, 0, 0, sub) for v in xo]
                high_x = [shift(v, -1, 0, 7, sub) for v in xo] if q else xo
                low_y = yo if p else [shift(v, 1, 1, 0, lane) for v in yo]
                high_y = [shift(v, -1, 1, 127, lane) for v in yo] if p else yo
                a, b, m = stencil_terms([low_z, low_x, low_y], [high_z, high_x, high_y], here, inside)
                if q:
                    b[1] = jnp.where(sub == 7, 0.0, b[1])
                else:
                    a[1] = jnp.where(sub == 0, 0.0, a[1])
                if p:
                    b[2] = jnp.where(lane == 127, 0.0, b[2])
                else:
                    a[2] = jnp.where(lane == 0, 0.0, a[2])
                for i, x in enumerate(a + b + m[0] + m[1] + m[2]):
                    coefs[l, k, i] = x
        return carry

    lax.fori_loop(1, NL - 1, build, 0)


def split_kernel(c_ref, u_ref, out_ref, ev, od):
    perm = lane_parity()
    for part, ref in ((0, c_ref), (1, u_ref)):
        both = jnp.dot(ref[...].reshape(192, 256), perm, precision=HI, preferred_element_type=F32)
        ev[part] = both[:, :128]
        od[part] = both[:, 128:]
        for q in range(2):
            for p, half in ((0, ev), (1, od)):
                got = half[part, pl.ds(q, 96, stride=2), :]
                out_ref[3 * part:3 * part + 3, :, 2 * q + p] = got.reshape(3, 4, 8, 128)


def split_fields(c, u):
    return pl.pallas_call(
        split_kernel,
        out_shape=shaped(6, 4, 4, 8, 128),
        in_specs=[VSPEC] * 2,
        out_specs=VSPEC,
        scratch_shapes=[pltpu.VMEM((2, 192, 128), F32)] * 2,
        compiler_params=pltpu.CompilerParams(vmem_limit_bytes=GRANT),
        cost_estimate=cost(50_000_000, 800_000),
        name="split",
    )(c, u)


def fine1_kernel(pos_ref, m1_ref, own_ref, p1_ref, start_ref, after_ref, speed, share_ref,
                 state_a, state_b, begin, coefs, share, sems):
    slab = pos_ref[0]
    depth = pos_ref[2]
    for i, ref in enumerate((m1_ref, own_ref, p1_ref)):
        state_a[:, 4 * i:4 * i + 4] = ref[0:3]
        begin[:, 4 * i:4 * i + 4] = ref[0:3]
        speed[:, 4 * i:4 * i + 4] = ref[3:6]
    keep = pltpu.make_async_copy(begin, start_ref, sems.at[0])
    keep.start()
    for j in (2, 3):
        for c, v in enumerate(restrict(speed, j)):
            for to in range(share.shape[0]):
                share[to, j - 2, c] = 2.0 * v
    send = pltpu.make_async_copy(share, share_ref, sems.at[1])
    send.start()
    fine_coefs(slab, depth, speed, coefs)
    march4(coefs, state_a, state_b)
    after_ref[...] = state_a[:, 4:8]
    keep.wait()
    send.wait()


def fine1(pos, m1, own, p1, slabs):
    return pl.pallas_call(
        fine1_kernel,
        out_shape=(shaped(3, NL, 4, 8, 128), shaped(3, 4, 4, 8, 128), shaped(3, NL, 4, 8, 128),
                   shaped(slabs, 2, 3, 8, 128)),
        in_specs=[SSPEC] + [VSPEC] * 3,
        out_specs=(HSPEC, VSPEC, VSPEC, HSPEC),
        scratch_shapes=[pltpu.VMEM((3, NL, 4, 8, 128), F32)] * 3 + [pltpu.VMEM((NL, 4, 15, 8, 128), F32)]
        + [pltpu.VMEM((slabs, 2, 3, 8, 128), F32), pltpu.SemaphoreType.DMA((2,))],
        compiler_params=pltpu.CompilerParams(vmem_limit_bytes=GRANT),
        cost_estimate=cost(10_000_000, 6_000_000),
        name="fine1",
    )(pos, m1, own, p1)


def fine2_kernel(pos_ref, speed, start_ref, m1_ref, own_ref, p1_ref, relaxed_ref, forcing_ref, state_a, state_b, coefs, sem):
    slab = pos_ref[0]
    first = pos_ref[1] == 1
    depth = pos_ref[2]
    @pl.when(first)
    def _():
        fetch = pltpu.make_async_copy(start_ref, state_a, sem)
        fetch.start()
        fetch.wait()

    @pl.when(jnp.logical_not(first))
    def _():
        for i, ref in enumerate((m1_ref, own_ref, p1_ref)):
            state_a[:, 4 * i:4 * i + 4] = ref[...]
    relaxed_ref[...] = state_a[:, 4:8]
    fine_coefs(slab, depth, speed, coefs)
    coarse = {j: restrict(state_a, j) for j in range(1, 5)}
    speed_c = {j: [2.0 * v for v in restrict(speed, j)] for j in range(1, 5)}
    image = {}
    for j in (2, 3):
        cc = {}
        coarse_coefs(*[speed_c[i] for i in (j - 1, j, j + 1)], jnp.float32(1.0), cc.__setitem__)
        image[j] = psi(cc.__getitem__, coarse[j - 1], coarse[j], coarse[j + 1])
    march4(coefs, state_a, state_b)
    for i, j in enumerate((2, 3)):
        again = restrict(state_a, j)
        for c in range(3):
            forcing = again[c] - image[j][c]
            forcing = forcing + jnp.where(first, image[j][c], 0.0)
            forcing_ref[i, c] = forcing


def fine2(pos, speed, start, m1, own, p1):
    return pl.pallas_call(
        fine2_kernel,
        out_shape=(shaped(3, 4, 4, 8, 128), shaped(2, 3, 8, 128)),
        in_specs=[SSPEC, VSPEC, HSPEC] + [VSPEC] * 3,
        out_specs=(VSPEC,) * 2,
        scratch_shapes=[pltpu.VMEM((3, NL, 4, 8, 128), F32)] * 2
        + [pltpu.VMEM((NL, 4, 15, 8, 128), F32), pltpu.SemaphoreType.DMA],
        compiler_params=pltpu.CompilerParams(vmem_limit_bytes=GRANT),
        cost_estimate=cost(10_000_000, 6_000_000),
        name="fine2",
    )(pos, speed, start, m1, own, p1)


def coefs_kernel(speed_ref, coefs):
    layers = speed_ref.shape[0]

    def one(j, carry):
        def at(i):
            keep = jnp.where(jnp.logical_and(i >= 0, i < layers), 1.0, 0.0).astype(F32)
            k = jnp.clip(i, 0, layers - 1)
            return [speed_ref[k, c] * keep for c in range(3)]

        def store(i, x):
            coefs[j, i] = x
        coarse_coefs(at(j - 1), at(j), at(j + 1), jnp.float32(1.0), store)
        return carry
    lax.fori_loop(0, layers, one, 0, unroll=2)


def sweep_coefs(speed):
    return pl.pallas_call(
        coefs_kernel,
        out_shape=shaped(speed.shape[0], 15, 8, 128),
        in_specs=[VSPEC],
        out_specs=VSPEC,
        compiler_params=pltpu.CompilerParams(vmem_limit_bytes=GRANT),
        cost_estimate=cost(3_000_000, 2_400_000),
        name="coefs",
    )(speed)


def window(slab, halo, layers):
    count = min(layers, 2 + 2 * halo)
    return count, jnp.clip(2 * slab - halo, 0, layers - count)


def psi_step(coefs, src, dst, chunk, low, high):
    def some(i, carry):
        for dj in range(chunk):
            j = i * chunk + dj
            new = psi(lambda n: coefs[j, n],
                      [src[j, c] for c in range(3)],
                      [src[j + 1, c] for c in range(3)],
                      [src[j + 2, c] for c in range(3)])
            for c in range(3):
                dst[j + 1, c] = new[c]
        return carry
    lax.fori_loop(low, high, some, 0)


def spread(distance, halo, slab, coefs, got_ref, state_a, state_b):
    layers = coefs.shape[0]
    for ref in (state_a, state_b):
        ref[...] = jnp.zeros_like(ref)
    n_in, at_in = window(slab, halo, layers)
    state_a[pl.ds(at_in + 1, n_in)] = got_ref[...]
    src, dst = state_a, state_b
    chunk = 2 if distance == 1 else 4
    for s in range(distance):
        reach = halo + 1 + s
        low = jnp.maximum(2 * slab - reach, 0) // chunk
        high = (jnp.minimum(2 * slab + 2 + reach, layers) + chunk - 1) // chunk
        psi_step(coefs, src, dst, chunk, low, high)
        src, dst = dst, src
    return src, dst


def round_kernel(distance, halo, pos_ref, coefs, own_ref, got_ref, out_ref, state_a, state_b):
    slab = pos_ref[0]
    layers = coefs.shape[0]
    n_in, at_in = window(slab, halo, layers)
    n_out, at_out = window(slab, halo + distance, layers)
    last, _ = spread(distance, halo, slab, coefs, got_ref, state_a, state_b)
    out_ref[...] = last[pl.ds(at_out + 1, n_out)]
    inner = pl.ds(at_in - at_out, n_in)
    out_ref[inner] = out_ref[inner] + own_ref[...]


def final_kernel(distance, halo, pos_ref, coefs, own_ref, got_ref, share_ref, state_a, state_b):
    slab = pos_ref[0]
    layers = coefs.shape[0]
    n_in, at_in = window(slab, halo, layers)
    last, other = spread(distance, halo, slab, coefs, got_ref, state_a, state_b)
    inner = pl.ds(at_in + 1, n_in)
    last[inner] = last[inner] + own_ref[...]
    share_ref[:, 0] = last[1:layers + 1].reshape(layers // 2, 2, 3, 8, 128)

    def pair(i, carry):
        psi_step(coefs, last, other, FULL_CHUNK, 0, layers // FULL_CHUNK)
        psi_step(coefs, other, last, FULL_CHUNK, 0, layers // FULL_CHUNK)
        return carry
    lax.fori_loop(0, distance, pair, 0)
    share_ref[:, 1] = last[1:layers + 1].reshape(layers // 2, 2, 3, 8, 128)


def sweep_round(distance, halo, final, pos, coefs, own, got):
    layers = coefs.shape[0]
    out = shaped(layers // 2, 2, 2, 3, 8, 128) if final else shaped(min(layers, 2 + 2 * (halo + distance)), 3, 8, 128)
    return pl.pallas_call(
        functools.partial(final_kernel if final else round_kernel, distance, halo),
        out_shape=out,
        in_specs=[SSPEC] + [VSPEC] * 3,
        out_specs=VSPEC,
        scratch_shapes=[pltpu.VMEM((layers + 2, 3, 8, 128), F32)] * 2,
        compiler_params=pltpu.CompilerParams(vmem_limit_bytes=GRANT),
        cost_estimate=cost((3 if final else 1) * distance * 2_000_000, 3_000_000),
    )(pos, coefs, own, got)


def total_kernel(got_ref, near_ref, far_ref):
    for i in range(2):
        for c in range(3):
            for part, ref in ((0, near_ref), (1, far_ref)):
                terms = [got_ref[s, part, i, c] for s in range(got_ref.shape[0])]
                while len(terms) > 1:
                    terms = [a + b for a, b in zip(terms[::2], terms[1::2])] + terms[len(terms) // 2 * 2:]
                ref[i, c] = terms[0]


def totals(got):
    return pl.pallas_call(
        total_kernel,
        out_shape=(shaped(2, 3, 8, 128),) * 2,
        in_specs=[VSPEC],
        out_specs=(VSPEC,) * 2,
        compiler_params=pltpu.CompilerParams(vmem_limit_bytes=GRANT),
        cost_estimate=cost(200_000, 850_000),
        name="totals",
    )(got)


def last_kernel(pos_ref, relaxed_ref, near_ref, far_ref, out_ref, ev, od):
    first = pos_ref[1] == 1
    for zc in range(2):
        for c in range(3):
            w = [[relaxed_ref[c, 2 * zc + dz, k] for k in range(4)] for dz in range(2)]
            lo, hi = [(v[0] + v[1]) + (v[2] + v[3]) for v in w]
            mean = (lo + hi) * 0.125
            diff = jnp.where(first, mean, near_ref[zc, c] + far_ref[zc, c]) - mean
            for dz in range(2):
                row0 = (c * 4 + 2 * zc + dz) * 16
                for q in range(2):
                    ev[pl.ds(row0 + q, 8, stride=2), :] = w[dz][2 * q] + diff
                    od[pl.ds(row0 + q, 8, stride=2), :] = w[dz][2 * q + 1] + diff
    both = jnp.concatenate([ev[...], od[...]], axis=1)
    out = jnp.dot(both, lane_parity(True), precision=HI, preferred_element_type=F32)
    out_ref[...] = out.reshape(3, 4, 16, 256)


def sweep_last(pos, relaxed, near, far):
    return pl.pallas_call(
        last_kernel,
        out_shape=shaped(3, 4, 16, 256),
        in_specs=[SSPEC] + [VSPEC] * 3,
        out_specs=VSPEC,
        scratch_shapes=[pltpu.VMEM((192, 128), F32)] * 2,
        compiler_params=pltpu.CompilerParams(vmem_limit_bytes=GRANT),
        cost_estimate=cost(2_000_000, 500_000),
        name="last",
    )(pos, relaxed, near, far)


def moved(block, by_t, by_z):
    nt, nz = lax.axis_size("tm"), lax.axis_size("gz")
    route = [
        ((t - by_t) * nz + z - by_z, t * nz + z)
        for t in range(nt) for z in range(nz)
        if 0 <= t - by_t < nt and 0 <= z - by_z < nz
    ]
    return lax.ppermute(block, ("tm", "gz"), route)


def local(c_states, velocity):
    slab = lax.axis_index("gz")
    t = lax.axis_index("tm")
    slabs = lax.axis_size("gz")
    depth = slabs * velocity.shape[1]
    pos = jnp.stack([slab, (t == 0).astype(jnp.int32), jnp.int32(depth)])
    own = split_fields(c_states[0], velocity)
    start, after, velocity_ext, share = fine1(pos, moved(own, 0, 1), own, moved(own, 0, -1), slabs)
    around = []
    for by in (1, 0, -1):
        around.append(moved(after, 1, by))
    speed = lax.all_to_all(share, "gz", 0, 0, tiled=True)
    relaxed, state = fine2(pos, velocity_ext, start, *around)
    coefs = sweep_coefs(speed.reshape(2 * slabs, 3, 8, 128))
    for distance in (1, 2, 4, 8):
        state = sweep_round(distance, distance - 1, distance == 8, pos, coefs, state, moved(state, distance, 0))
    near, far = totals(lax.all_to_all(state, "gz", 0, 0, tiled=True))
    out = sweep_last(pos, relaxed, moved(near, 1, 0), moved(far, 17, 0))
    return out[None]


def solution(mesh):
    return jax.shard_map(
        local,
        mesh=mesh,
        in_specs=(P("tm", None, "gz", None, None), P(None, "gz", None, None)),
        out_specs=P("tm", None, "gz", None, None),
        check_vma=False,
    )
```

```python
import functools
import jax
import jax.numpy as jnp
from jax import lax
from jax.experimental import pallas as pl
from jax.experimental.pallas import tpu as pltpu
from jax.sharding import PartitionSpec as P


STEPS = 4
KAPPA = 0.04
FINE_UNROLL = 2
FULL_CHUNK = 8
F32 = jnp.float32
HI = lax.Precision.HIGHEST
VM = pltpu.MemorySpace.VMEM


def lane_parity(transpose=False):
    row = lax.broadcasted_iota(jnp.int32, (256, 256), 1 if transpose else 0)
    col = lax.broadcasted_iota(jnp.int32, (256, 256), 0 if transpose else 1)
    want = 2 * (col % 128) + col // 128
    return (row == want).astype(F32)


def shift(v, by, axis, masked_at, index):
    return jnp.where(index == masked_at, 0.0, pltpu.roll(v, by % v.shape[axis], axis))


def stencil_terms(low, high, mid, inside):
    a = [KAPPA + jnp.maximum(mid[d], 0.0) for d in range(3)]
    b = [KAPPA - jnp.minimum(mid[d], 0.0) for d in range(3)]
    centre = 1.0 - (a[0] + b[0] + a[1] + b[1] + a[2] + b[2])
    m = [[(high[e][c] - low[e][c]) * 0.5 for e in range(3)] for c in range(3)]
    for c in range(3):
        m[c][c] = m[c][c] + centre
    a = [x * inside for x in a]
    b = [x * inside for x in b]
    m = [[x * inside for x in row] for row in m]
    return a, b, m


def iotas():
    sub = lax.broadcasted_iota(jnp.int32, (8, 128), 0)
    lane = lax.broadcasted_iota(jnp.int32, (8, 128), 1)
    return sub, lane


def coarse_coefs(below, here, above, inside, store):
    sub, lane = iotas()
    low = [below, [shift(v, 1, 0, 0, sub) for v in here], [shift(v, 1, 1, 0, lane) for v in here]]
    high = [above, [shift(v, -1, 0, 7, sub) for v in here], [shift(v, -1, 1, 127, lane) for v in here]]
    a, b, m = stencil_terms(low, high, here, inside)
    a[1] = jnp.where(sub == 0, 0.0, a[1])
    b[1] = jnp.where(sub == 7, 0.0, b[1])
    a[2] = jnp.where(lane == 0, 0.0, a[2])
    b[2] = jnp.where(lane == 127, 0.0, b[2])
    flat = a + b + m[0] + m[1] + m[2]
    for i, x in enumerate(flat):
        store(i, x)


def psi(coef, below, here, above):
    a = [coef(i) for i in range(3)]
    b = [coef(3 + i) for i in range(3)]
    out = []
    for c in range(3):
        w = here[c]
        acc = a[0] * below[c] + b[0] * above[c]
        acc = acc + (a[1] * pltpu.roll(w, 1, 0) + b[1] * pltpu.roll(w, 7, 0))
        acc = acc + (a[2] * pltpu.roll(w, 1, 1) + b[2] * pltpu.roll(w, 127, 1))
        acc = acc + (coef(6 + 3 * c) * here[0] + coef(7 + 3 * c) * here[1] + coef(8 + 3 * c) * here[2])
        out.append(acc)
    return out


NL = 12
VSPEC = pl.BlockSpec(memory_space=VM)
HSPEC = pl.BlockSpec(memory_space=pltpu.MemorySpace.HBM)
SSPEC = pl.BlockSpec(memory_space=pltpu.MemorySpace.SMEM)
PARAMS = pltpu.CompilerParams(vmem_limit_bytes=16 << 20)


def shaped(*dims):
    return jax.ShapeDtypeStruct(dims, F32)


def cost(flops, moved):
    return pl.CostEstimate(flops=flops, bytes_accessed=moved, transcendentals=0)


def march4(coefs, first, second):
    src, dst = first, second
    for k in range(1, STEPS + 1):
        def layer(l, carry, src=src, dst=dst):
            w = [[src[c, l, k] for k in range(4)] for c in range(3)]
            for q in range(2):
                for p in range(2):
                    k = 2 * q + p
                    kx = 2 * (1 - q) + p
                    ky = 2 * q + 1 - p
                    cf = [coefs[l, k, i] for i in range(15)]
                    for c in range(3):
                        xo = w[c][kx]
                        xr = pltpu.roll(xo, 7 if q else 1, 0)
                        yo = w[c][ky]
                        yr = pltpu.roll(yo, 127 if p else 1, 1)
                        acc = cf[0] * src[c, l - 1, k] + cf[3] * src[c, l + 1, k]
                        acc = acc + (cf[1] * (xo if q else xr) + cf[4] * (xr if q else xo))
                        acc = acc + (cf[2] * (yo if p else yr) + cf[5] * (yr if p else yo))
                        acc = acc + (cf[6 + 3 * c] * w[0][k] + cf[7 + 3 * c] * w[1][k] + cf[8 + 3 * c] * w[2][k])
                        dst[c, l, k] = acc
            return carry
        lax.fori_loop(k, NL - k, layer, 0, unroll=FINE_UNROLL)
        src, dst = dst, src


def restrict(src, j):
    out = []
    for c in range(3):
        lo = (src[c, 2 * j, 0] + src[c, 2 * j, 1]) + (src[c, 2 * j, 2] + src[c, 2 * j, 3])
        hi = (src[c, 2 * j + 1, 0] + src[c, 2 * j + 1, 1]) + (src[c, 2 * j + 1, 2] + src[c, 2 * j + 1, 3])
        out.append((lo + hi) * 0.125)
    return out


def fine_coefs(slab, depth, speed, coefs):
    sub, lane = iotas()

    def build(l, carry):
        z = slab * 4 + l - 4
        inside = jnp.where(jnp.logical_and(z >= 0, z < depth), 1.0, 0.0).astype(F32)
        mid = [[speed[c, l, k] for c in range(3)] for k in range(4)]
        for q in range(2):
            for p in range(2):
                k = 2 * q + p
                here = mid[k]
                xo = mid[2 * (1 - q) + p]
                yo = mid[2 * q + 1 - p]
                low_z = [speed[c, l - 1, k] for c in range(3)]
                high_z = [speed[c, l + 1, k] for c in range(3)]
                low_x = xo if q else [shift(v, 1, 0, 0, sub) for v in xo]
                high_x = [shift(v, -1, 0, 7, sub) for v in xo] if q else xo
                low_y = yo if p else [shift(v, 1, 1, 0, lane) for v in yo]
                high_y = [shift(v, -1, 1, 127, lane) for v in yo] if p else yo
                a, b, m = stencil_terms([low_z, low_x, low_y], [high_z, high_x, high_y], here, inside)
                if q:
                    b[1] = jnp.where(sub == 7, 0.0, b[1])
                else:
                    a[1] = jnp.where(sub == 0, 0.0, a[1])
                if p:
                    b[2] = jnp.where(lane == 127, 0.0, b[2])
                else:
                    a[2] = jnp.where(lane == 0, 0.0, a[2])
                for i, x in enumerate(a + b + m[0] + m[1] + m[2]):
                    coefs[l, k, i] = x
        return carry

    lax.fori_loop(1, NL - 1, build, 0)


def split_kernel(c_ref, u_ref, out_ref, ev, od):
    perm = lane_parity()
    for part, ref in ((0, c_ref), (1, u_ref)):
        both = jnp.dot(ref[...].reshape(192, 256), perm, precision=HI, preferred_element_type=F32)
        ev[part] = both[:, :128]
        od[part] = both[:, 128:]
        for q in range(2):
            for p, half in ((0, ev), (1, od)):
                got = half[part, pl.ds(q, 96, stride=2), :]
                out_ref[3 * part:3 * part + 3, :, 2 * q + p] = got.reshape(3, 4, 8, 128)


def split_fields(c, u):
    return pl.pallas_call(
        split_kernel,
        out_shape=shaped(6, 4, 4, 8, 128),
        in_specs=[VSPEC] * 2,
        out_specs=VSPEC,
        scratch_shapes=[pltpu.VMEM((2, 192, 128), F32)] * 2,
        compiler_params=PARAMS,
        cost_estimate=cost(50_000_000, 800_000),
        name="split",
    )(c, u)


def fine1_kernel(pos_ref, m1_ref, own_ref, p1_ref, start_ref, after_ref, speed, share_ref,
                 state_a, state_b, begin, coefs, share, sems):
    slab = pos_ref[0]
    depth = pos_ref[2]
    for i, ref in enumerate((m1_ref, own_ref, p1_ref)):
        state_a[:, 4 * i:4 * i + 4] = ref[0:3]
        begin[:, 4 * i:4 * i + 4] = ref[0:3]
        speed[:, 4 * i:4 * i + 4] = ref[3:6]
    keep = pltpu.make_async_copy(begin, start_ref, sems.at[0])
    keep.start()
    for j in (2, 3):
        for c, v in enumerate(restrict(speed, j)):
            for to in range(share.shape[0]):
                share[to, j - 2, c] = 2.0 * v
    send = pltpu.make_async_copy(share, share_ref, sems.at[1])
    send.start()
    fine_coefs(slab, depth, speed, coefs)
    march4(coefs, state_a, state_b)
    after_ref[...] = state_a[:, 4:8]
    keep.wait()
    send.wait()


def fine1(pos, m1, own, p1, slabs):
    return pl.pallas_call(
        fine1_kernel,
        out_shape=(shaped(3, NL, 4, 8, 128), shaped(3, 4, 4, 8, 128), shaped(3, NL, 4, 8, 128),
                   shaped(slabs, 2, 3, 8, 128)),
        in_specs=[SSPEC] + [VSPEC] * 3,
        out_specs=(HSPEC, VSPEC, VSPEC, HSPEC),
        scratch_shapes=[pltpu.VMEM((3, NL, 4, 8, 128), F32)] * 3 + [pltpu.VMEM((NL, 4, 15, 8, 128), F32)]
        + [pltpu.VMEM((slabs, 2, 3, 8, 128), F32), pltpu.SemaphoreType.DMA((2,))],
        compiler_params=PARAMS,
        cost_estimate=cost(10_000_000, 6_000_000),
        name="fine1",
    )(pos, m1, own, p1)


def fine2_kernel(pos_ref, speed, start_ref, m1_ref, own_ref, p1_ref, relaxed_ref, forcing_ref, state_a, state_b, coefs, sem):
    slab = pos_ref[0]
    first = pos_ref[1] == 1
    depth = pos_ref[2]
    @pl.when(first)
    def _():
        fetch = pltpu.make_async_copy(start_ref, state_a, sem)
        fetch.start()
        fetch.wait()

    @pl.when(jnp.logical_not(first))
    def _():
        for i, ref in enumerate((m1_ref, own_ref, p1_ref)):
            state_a[:, 4 * i:4 * i + 4] = ref[...]
    relaxed_ref[...] = state_a[:, 4:8]
    fine_coefs(slab, depth, speed, coefs)
    coarse = {j: restrict(state_a, j) for j in range(1, 5)}
    speed_c = {j: [2.0 * v for v in restrict(speed, j)] for j in range(1, 5)}
    image = {}
    for j in (2, 3):
        cc = {}
        coarse_coefs(*[speed_c[i] for i in (j - 1, j, j + 1)], jnp.float32(1.0), cc.__setitem__)
        image[j] = psi(cc.__getitem__, coarse[j - 1], coarse[j], coarse[j + 1])
    march4(coefs, state_a, state_b)
    for i, j in enumerate((2, 3)):
        again = restrict(state_a, j)
        for c in range(3):
            forcing = again[c] - image[j][c]
            forcing = forcing + jnp.where(first, image[j][c], 0.0)
            forcing_ref[i, c] = forcing


def fine2(pos, speed, start, m1, own, p1):
    return pl.pallas_call(
        fine2_kernel,
        out_shape=(shaped(3, 4, 4, 8, 128), shaped(2, 3, 8, 128)),
        in_specs=[SSPEC, VSPEC, HSPEC] + [VSPEC] * 3,
        out_specs=(VSPEC,) * 2,
        scratch_shapes=[pltpu.VMEM((3, NL, 4, 8, 128), F32)] * 2
        + [pltpu.VMEM((NL, 4, 15, 8, 128), F32), pltpu.SemaphoreType.DMA],
        compiler_params=PARAMS,
        cost_estimate=cost(10_000_000, 6_000_000),
        name="fine2",
    )(pos, speed, start, m1, own, p1)


def layer_coefs(speed_ref, j, store):
    layers = speed_ref.shape[0]

    def at(i):
        keep = jnp.where(jnp.logical_and(i >= 0, i < layers), 1.0, 0.0).astype(F32)
        k = jnp.clip(i, 0, layers - 1)
        return [speed_ref[k, c] * keep for c in range(3)]
    coarse_coefs(at(j - 1), at(j), at(j + 1), jnp.float32(1.0), store)


def coefs_kernel(speed_ref, coefs):
    def one(j, carry):
        def store(i, x):
            coefs[j, i] = x
        layer_coefs(speed_ref, j, store)
        return carry
    lax.fori_loop(0, speed_ref.shape[0], one, 0, unroll=2)


def sweep_coefs(speed):
    return pl.pallas_call(
        coefs_kernel,
        out_shape=shaped(speed.shape[0], 15, 8, 128),
        in_specs=[VSPEC],
        out_specs=VSPEC,
        compiler_params=PARAMS,
        cost_estimate=cost(3_000_000, 2_400_000),
        name="coefs",
    )(speed)


def window(slab, halo, layers):
    count = min(layers, 2 + 2 * halo)
    return count, jnp.clip(2 * slab - halo, 0, layers - count)


def psi_step(coefs, src, dst, chunk, low, high):
    def some(i, carry):
        for dj in range(chunk):
            j = i * chunk + dj
            new = psi(lambda n: coefs[j, n],
                      [src[j, c] for c in range(3)],
                      [src[j + 1, c] for c in range(3)],
                      [src[j + 2, c] for c in range(3)])
            for c in range(3):
                dst[j + 1, c] = new[c]
        return carry
    lax.fori_loop(low, high, some, 0)


def first_kernel(pos_ref, speed_ref, near_ref, far_ref, out_ref, state, coefs):
    slab = pos_ref[0]
    n_out, at_out = window(slab, 1, speed_ref.shape[0])
    state[...] = jnp.zeros_like(state)
    inner = 2 * slab - at_out
    state[pl.ds(inner + 1, 2)] = far_ref[...]
    for i in range(n_out):
        def store(n, x, i=i):
            coefs[i, n] = x
        layer_coefs(speed_ref, at_out + i, store)
        new = psi(lambda n, i=i: coefs[i, n], *[[state[i + d, c] for c in range(3)] for d in range(3)])
        for c in range(3):
            out_ref[i, c] = new[c]
    out_ref[pl.ds(inner, 2)] = out_ref[pl.ds(inner, 2)] + near_ref[...]


def first_round(pos, speed, near, far):
    return pl.pallas_call(
        first_kernel,
        out_shape=shaped(4, 3, 8, 128),
        in_specs=[SSPEC] + [VSPEC] * 3,
        out_specs=VSPEC,
        scratch_shapes=[pltpu.VMEM((6, 3, 8, 128), F32), pltpu.VMEM((4, 15, 8, 128), F32)],
        compiler_params=PARAMS,
        cost_estimate=cost(1_000_000, 500_000),
        name="round1",
    )(pos, speed, near, far)


def spread(distance, halo, slab, coefs, got_ref, state_a, state_b):
    layers = coefs.shape[0]
    for ref in (state_a, state_b):
        ref[...] = jnp.zeros_like(ref)
    n_in, at_in = window(slab, halo, layers)
    state_a[pl.ds(at_in + 1, n_in)] = got_ref[...]
    src, dst = state_a, state_b
    chunk = 2 if distance == 1 else 4
    for s in range(distance):
        reach = halo + 1 + s
        low = jnp.maximum(2 * slab - reach, 0) // chunk
        high = (jnp.minimum(2 * slab + 2 + reach, layers) + chunk - 1) // chunk
        psi_step(coefs, src, dst, chunk, low, high)
        src, dst = dst, src
    return src, dst


def round_kernel(distance, halo, pos_ref, coefs, own_ref, got_ref, out_ref, state_a, state_b):
    slab = pos_ref[0]
    layers = coefs.shape[0]
    n_in, at_in = window(slab, halo, layers)
    n_out, at_out = window(slab, halo + distance, layers)
    last, _ = spread(distance, halo, slab, coefs, got_ref, state_a, state_b)
    out_ref[...] = last[pl.ds(at_out + 1, n_out)]
    inner = pl.ds(at_in - at_out, n_in)
    out_ref[inner] = out_ref[inner] + own_ref[...]


def final_kernel(distance, halo, pos_ref, coefs, own_ref, got_ref, share_ref, state_a, state_b):
    slab = pos_ref[0]
    layers = coefs.shape[0]
    n_in, at_in = window(slab, halo, layers)
    last, other = spread(distance, halo, slab, coefs, got_ref, state_a, state_b)
    inner = pl.ds(at_in + 1, n_in)
    last[inner] = last[inner] + own_ref[...]
    share_ref[:, 0] = last[1:layers + 1].reshape(layers // 2, 2, 3, 8, 128)

    def pair(i, carry):
        psi_step(coefs, last, other, FULL_CHUNK, 0, layers // FULL_CHUNK)
        psi_step(coefs, other, last, FULL_CHUNK, 0, layers // FULL_CHUNK)
        return carry
    lax.fori_loop(0, distance, pair, 0)
    share_ref[:, 1] = last[1:layers + 1].reshape(layers // 2, 2, 3, 8, 128)


def sweep_round(distance, halo, final, pos, coefs, own, got):
    layers = coefs.shape[0]
    out = shaped(layers // 2, 2, 2, 3, 8, 128) if final else shaped(min(layers, 2 + 2 * (halo + distance)), 3, 8, 128)
    return pl.pallas_call(
        functools.partial(final_kernel if final else round_kernel, distance, halo),
        out_shape=out,
        in_specs=[SSPEC] + [VSPEC] * 3,
        out_specs=VSPEC,
        scratch_shapes=[pltpu.VMEM((layers + 2, 3, 8, 128), F32)] * 2,
        compiler_params=PARAMS,
        cost_estimate=cost((3 if final else 1) * distance * 2_000_000, 3_000_000),
    )(pos, coefs, own, got)


def total_kernel(got_ref, near_ref, far_ref):
    for i in range(2):
        for c in range(3):
            for part, ref in ((0, near_ref), (1, far_ref)):
                terms = [got_ref[s, part, i, c] for s in range(got_ref.shape[0])]
                while len(terms) > 1:
                    terms = [a + b for a, b in zip(terms[::2], terms[1::2])] + terms[len(terms) // 2 * 2:]
                ref[i, c] = terms[0]


def totals(got):
    return pl.pallas_call(
        total_kernel,
        out_shape=(shaped(2, 3, 8, 128),) * 2,
        in_specs=[VSPEC],
        out_specs=(VSPEC,) * 2,
        compiler_params=PARAMS,
        cost_estimate=cost(200_000, 850_000),
        name="totals",
    )(got)


def base_kernel(relaxed_ref, base_ref, mean_ref, ev, od):
    for zc in range(2):
        for c in range(3):
            w = [[relaxed_ref[c, 2 * zc + dz, k] for k in range(4)] for dz in range(2)]
            lo, hi = [(v[0] + v[1]) + (v[2] + v[3]) for v in w]
            mean = (lo + hi) * 0.125
            mean_ref[zc, c] = mean
            for dz in range(2):
                row0 = (c * 4 + 2 * zc + dz) * 16
                for q in range(2):
                    ev[pl.ds(row0 + q, 8, stride=2), :] = w[dz][2 * q] - mean
                    od[pl.ds(row0 + q, 8, stride=2), :] = w[dz][2 * q + 1] - mean
    both = jnp.concatenate([ev[...], od[...]], axis=1)
    out = jnp.dot(both, lane_parity(True), precision=HI, preferred_element_type=F32)
    base_ref[...] = out.reshape(3, 4, 16, 256)


def output_base(relaxed):
    return pl.pallas_call(
        base_kernel,
        out_shape=(shaped(3, 4, 16, 256), shaped(2, 3, 8, 128)),
        in_specs=[VSPEC],
        out_specs=(VSPEC,) * 2,
        scratch_shapes=[pltpu.VMEM((192, 128), F32)] * 2,
        compiler_params=PARAMS,
        cost_estimate=cost(25_000_000, 400_000),
        name="base",
    )(relaxed)


def last_kernel(pos_ref, base_ref, mean_ref, near_ref, far_ref, out_ref, half_a, half_b):
    first = pos_ref[1] == 1
    row = lax.broadcasted_iota(jnp.int32, (128, 256), 0)
    col = lax.broadcasted_iota(jnp.int32, (128, 256), 1)
    widen = (col // 2 == row).astype(F32)
    coarse = jnp.where(first, mean_ref[...], near_ref[...] + far_ref[...]).reshape(48, 128)
    wide = jnp.dot(coarse, widen, precision=HI, preferred_element_type=F32)
    for n in range(6):
        for h, half in ((0, half_a), (1, half_b)):
            piece = wide[8 * n:8 * n + 8, 128 * h:128 * h + 128]
            for q in range(2):
                half[pl.ds(16 * n + q, 8, stride=2), :] = piece
    for zc in range(2):
        for c in range(3):
            n = 3 * zc + c
            for h, half in ((0, half_a), (1, half_b)):
                piece = half[16 * n:16 * n + 16, :]
                lanes = slice(128 * h, 128 * h + 128)
                for dz in range(2):
                    out_ref[c, 2 * zc + dz, :, lanes] = base_ref[c, 2 * zc + dz, :, lanes] + piece


def sweep_last(pos, base, mean, near, far):
    return pl.pallas_call(
        last_kernel,
        out_shape=shaped(3, 4, 16, 256),
        in_specs=[SSPEC] + [VSPEC] * 4,
        out_specs=VSPEC,
        scratch_shapes=[pltpu.VMEM((96, 128), F32)] * 2,
        compiler_params=PARAMS,
        cost_estimate=cost(2_000_000, 500_000),
        name="last",
    )(pos, base, mean, near, far)


def moved(block, by_t, by_z):
    nt, nz = lax.axis_size("tm"), lax.axis_size("gz")
    route = [
        ((t - by_t) * nz + z - by_z, t * nz + z)
        for t in range(nt) for z in range(nz)
        if 0 <= t - by_t < nt and 0 <= z - by_z < nz
    ]
    return lax.ppermute(block, ("tm", "gz"), route)


def local(c_states, velocity):
    slab = lax.axis_index("gz")
    t = lax.axis_index("tm")
    slabs = lax.axis_size("gz")
    depth = slabs * velocity.shape[1]
    pos = jnp.stack([slab, (t == 0).astype(jnp.int32), jnp.int32(depth)])
    own = split_fields(c_states[0], velocity)
    start, after, velocity_ext, share = fine1(pos, moved(own, 0, 1), own, moved(own, 0, -1), slabs)
    around = []
    for by in (1, 0, -1):
        around.append(moved(after, 1, by))
    speed = lax.all_to_all(share, "gz", 0, 0, tiled=True)
    relaxed, state = fine2(pos, velocity_ext, start, *around)
    base, mean = output_base(relaxed)
    speed = speed.reshape(2 * slabs, 3, 8, 128)
    coefs = sweep_coefs(speed)
    state = first_round(pos, speed, moved(state, 1, 0), moved(state, 2, 0))
    for distance in (2, 4, 8):
        state = sweep_round(distance, distance - 1, distance == 8, pos, coefs, state, moved(state, distance, 0))
    near, far = totals(lax.all_to_all(state, "gz", 0, 0, tiled=True))
    out = sweep_last(pos, base, mean, near, moved(far, 16, 0))
    return out[None]


def solution(mesh):
    return jax.shard_map(
        local,
        mesh=mesh,
        in_specs=(P("tm", None, "gz", None, None), P(None, "gz", None, None)),
        out_specs=P("tm", None, "gz", None, None),
        check_vma=False,
    )
```

```python
import functools
import jax
import jax.numpy as jnp
from jax import lax
from jax.experimental import pallas as pl
from jax.experimental.pallas import tpu as pltpu
from jax.sharding import PartitionSpec as P


STEPS = 4
KAPPA = 0.04
FINE_UNROLL = 2
FULL_CHUNK = 32
F32 = jnp.float32
HI = lax.Precision.HIGHEST
VM = pltpu.MemorySpace.VMEM


def lane_parity(transpose=False):
    row = lax.broadcasted_iota(jnp.int32, (256, 256), 1 if transpose else 0)
    col = lax.broadcasted_iota(jnp.int32, (256, 256), 0 if transpose else 1)
    want = 2 * (col % 128) + col // 128
    return (row == want).astype(F32)


def shift(v, by, axis, masked_at, index):
    return jnp.where(index == masked_at, 0.0, pltpu.roll(v, by % v.shape[axis], axis))


def stencil_terms(low, high, mid, inside):
    a = [KAPPA + jnp.maximum(mid[d], 0.0) for d in range(3)]
    b = [KAPPA - jnp.minimum(mid[d], 0.0) for d in range(3)]
    centre = 1.0 - (a[0] + b[0] + a[1] + b[1] + a[2] + b[2])
    m = [[(high[e][c] - low[e][c]) * 0.5 for e in range(3)] for c in range(3)]
    for c in range(3):
        m[c][c] = m[c][c] + centre
    a = [x * inside for x in a]
    b = [x * inside for x in b]
    m = [[x * inside for x in row] for row in m]
    return a, b, m


def iotas():
    sub = lax.broadcasted_iota(jnp.int32, (8, 128), 0)
    lane = lax.broadcasted_iota(jnp.int32, (8, 128), 1)
    return sub, lane


def coarse_coefs(below, here, above, inside, store):
    sub, lane = iotas()
    low = [below, [shift(v, 1, 0, 0, sub) for v in here], [shift(v, 1, 1, 0, lane) for v in here]]
    high = [above, [shift(v, -1, 0, 7, sub) for v in here], [shift(v, -1, 1, 127, lane) for v in here]]
    a, b, m = stencil_terms(low, high, here, inside)
    a[1] = jnp.where(sub == 0, 0.0, a[1])
    b[1] = jnp.where(sub == 7, 0.0, b[1])
    a[2] = jnp.where(lane == 0, 0.0, a[2])
    b[2] = jnp.where(lane == 127, 0.0, b[2])
    flat = a + b + m[0] + m[1] + m[2]
    for i, x in enumerate(flat):
        store(i, x)


def psi(coef, below, here, above):
    a = [coef(i) for i in range(3)]
    b = [coef(3 + i) for i in range(3)]
    out = []
    for c in range(3):
        w = here[c]
        acc = a[0] * below[c] + b[0] * above[c]
        acc = acc + (a[1] * pltpu.roll(w, 1, 0) + b[1] * pltpu.roll(w, 7, 0))
        acc = acc + (a[2] * pltpu.roll(w, 1, 1) + b[2] * pltpu.roll(w, 127, 1))
        acc = acc + (coef(6 + 3 * c) * here[0] + coef(7 + 3 * c) * here[1] + coef(8 + 3 * c) * here[2])
        out.append(acc)
    return out


NL = 12
VSPEC = pl.BlockSpec(memory_space=VM)
HSPEC = pl.BlockSpec(memory_space=pltpu.MemorySpace.HBM)
SSPEC = pl.BlockSpec(memory_space=pltpu.MemorySpace.SMEM)
PARAMS = pltpu.CompilerParams(vmem_limit_bytes=16 << 20)


def shaped(*dims):
    return jax.ShapeDtypeStruct(dims, F32)


def cost(flops, moved):
    return pl.CostEstimate(flops=flops, bytes_accessed=moved, transcendentals=0)


def march4(coefs, first, second):
    src, dst = first, second
    for k in range(1, STEPS + 1):
        def layer(l, carry, src=src, dst=dst):
            w = [[src[c, l, k] for k in range(4)] for c in range(3)]
            for q in range(2):
                for p in range(2):
                    k = 2 * q + p
                    kx = 2 * (1 - q) + p
                    ky = 2 * q + 1 - p
                    cf = [coefs[l, k, i] for i in range(15)]
                    for c in range(3):
                        xo = w[c][kx]
                        xr = pltpu.roll(xo, 7 if q else 1, 0)
                        yo = w[c][ky]
                        yr = pltpu.roll(yo, 127 if p else 1, 1)
                        acc = cf[0] * src[c, l - 1, k] + cf[3] * src[c, l + 1, k]
                        acc = acc + (cf[1] * (xo if q else xr) + cf[4] * (xr if q else xo))
                        acc = acc + (cf[2] * (yo if p else yr) + cf[5] * (yr if p else yo))
                        acc = acc + (cf[6 + 3 * c] * w[0][k] + cf[7 + 3 * c] * w[1][k] + cf[8 + 3 * c] * w[2][k])
                        dst[c, l, k] = acc
            return carry
        lax.fori_loop(k, NL - k, layer, 0, unroll=FINE_UNROLL)
        src, dst = dst, src


def restrict(src, j):
    out = []
    for c in range(3):
        lo = (src[c, 2 * j, 0] + src[c, 2 * j, 1]) + (src[c, 2 * j, 2] + src[c, 2 * j, 3])
        hi = (src[c, 2 * j + 1, 0] + src[c, 2 * j + 1, 1]) + (src[c, 2 * j + 1, 2] + src[c, 2 * j + 1, 3])
        out.append((lo + hi) * 0.125)
    return out


def fine_coefs(slab, depth, speed, coefs):
    sub, lane = iotas()

    def build(l, carry):
        z = slab * 4 + l - 4
        inside = jnp.where(jnp.logical_and(z >= 0, z < depth), 1.0, 0.0).astype(F32)
        mid = [[speed[c, l, k] for c in range(3)] for k in range(4)]
        for q in range(2):
            for p in range(2):
                k = 2 * q + p
                here = mid[k]
                xo = mid[2 * (1 - q) + p]
                yo = mid[2 * q + 1 - p]
                low_z = [speed[c, l - 1, k] for c in range(3)]
                high_z = [speed[c, l + 1, k] for c in range(3)]
                low_x = xo if q else [shift(v, 1, 0, 0, sub) for v in xo]
                high_x = [shift(v, -1, 0, 7, sub) for v in xo] if q else xo
                low_y = yo if p else [shift(v, 1, 1, 0, lane) for v in yo]
                high_y = [shift(v, -1, 1, 127, lane) for v in yo] if p else yo
                a, b, m = stencil_terms([low_z, low_x, low_y], [high_z, high_x, high_y], here, inside)
                if q:
                    b[1] = jnp.where(sub == 7, 0.0, b[1])
                else:
                    a[1] = jnp.where(sub == 0, 0.0, a[1])
                if p:
                    b[2] = jnp.where(lane == 127, 0.0, b[2])
                else:
                    a[2] = jnp.where(lane == 0, 0.0, a[2])
                for i, x in enumerate(a + b + m[0] + m[1] + m[2]):
                    coefs[l, k, i] = x
        return carry

    lax.fori_loop(1, NL - 1, build, 0)


def split_kernel(c_ref, u_ref, out_ref, ev, od):
    perm = lane_parity()
    for part, ref in ((0, c_ref), (1, u_ref)):
        both = jnp.dot(ref[...].reshape(192, 256), perm, precision=HI, preferred_element_type=F32)
        ev[part] = both[:, :128]
        od[part] = both[:, 128:]
        for q in range(2):
            for p, half in ((0, ev), (1, od)):
                got = half[part, pl.ds(q, 96, stride=2), :]
                out_ref[3 * part:3 * part + 3, :, 2 * q + p] = got.reshape(3, 4, 8, 128)


def split_fields(c, u):
    return pl.pallas_call(
        split_kernel,
        out_shape=shaped(6, 4, 4, 8, 128),
        in_specs=[VSPEC] * 2,
        out_specs=VSPEC,
        scratch_shapes=[pltpu.VMEM((2, 192, 128), F32)] * 2,
        compiler_params=PARAMS,
        cost_estimate=cost(50_000_000, 800_000),
        name="split",
    )(c, u)


def fine1_kernel(pos_ref, m1_ref, own_ref, p1_ref, start_ref, after_ref, speed, share_ref,
                 state_a, state_b, begin, coefs, share, sems):
    slab = pos_ref[0]
    depth = pos_ref[2]
    for i, ref in enumerate((m1_ref, own_ref, p1_ref)):
        state_a[:, 4 * i:4 * i + 4] = ref[0:3]
        begin[:, 4 * i:4 * i + 4] = ref[0:3]
        speed[:, 4 * i:4 * i + 4] = ref[3:6]
    keep = pltpu.make_async_copy(begin, start_ref, sems.at[0])
    keep.start()
    for j in (2, 3):
        for c, v in enumerate(restrict(speed, j)):
            for to in range(share.shape[0]):
                share[to, j - 2, c] = 2.0 * v
    send = pltpu.make_async_copy(share, share_ref, sems.at[1])
    send.start()
    fine_coefs(slab, depth, speed, coefs)
    march4(coefs, state_a, state_b)
    after_ref[...] = state_a[:, 4:8]
    keep.wait()
    send.wait()


def fine1(pos, m1, own, p1, slabs):
    return pl.pallas_call(
        fine1_kernel,
        out_shape=(shaped(3, NL, 4, 8, 128), shaped(3, 4, 4, 8, 128), shaped(3, NL, 4, 8, 128),
                   shaped(slabs, 2, 3, 8, 128)),
        in_specs=[SSPEC] + [VSPEC] * 3,
        out_specs=(HSPEC, VSPEC, VSPEC, HSPEC),
        scratch_shapes=[pltpu.VMEM((3, NL, 4, 8, 128), F32)] * 3 + [pltpu.VMEM((NL, 4, 15, 8, 128), F32)]
        + [pltpu.VMEM((slabs, 2, 3, 8, 128), F32), pltpu.SemaphoreType.DMA((2,))],
        compiler_params=PARAMS,
        cost_estimate=cost(10_000_000, 6_000_000),
        name="fine1",
    )(pos, m1, own, p1)


def fine2_kernel(pos_ref, speed, start_ref, m1_ref, own_ref, p1_ref, relaxed_ref, forcing_ref, state_a, state_b, coefs, sem):
    slab = pos_ref[0]
    first = pos_ref[1] == 1
    depth = pos_ref[2]
    @pl.when(first)
    def _():
        fetch = pltpu.make_async_copy(start_ref, state_a, sem)
        fetch.start()
        fetch.wait()

    @pl.when(jnp.logical_not(first))
    def _():
        for i, ref in enumerate((m1_ref, own_ref, p1_ref)):
            state_a[:, 4 * i:4 * i + 4] = ref[...]
    relaxed_ref[...] = state_a[:, 4:8]
    fine_coefs(slab, depth, speed, coefs)
    coarse = {j: restrict(state_a, j) for j in range(1, 5)}
    speed_c = {j: [2.0 * v for v in restrict(speed, j)] for j in range(1, 5)}
    image = {}
    for j in (2, 3):
        cc = {}
        coarse_coefs(*[speed_c[i] for i in (j - 1, j, j + 1)], jnp.float32(1.0), cc.__setitem__)
        image[j] = psi(cc.__getitem__, coarse[j - 1], coarse[j], coarse[j + 1])
    march4(coefs, state_a, state_b)
    for i, j in enumerate((2, 3)):
        again = restrict(state_a, j)
        for c in range(3):
            forcing = again[c] - image[j][c]
            forcing = forcing + jnp.where(first, image[j][c], 0.0)
            forcing_ref[i, c] = forcing


def fine2(pos, speed, start, m1, own, p1):
    return pl.pallas_call(
        fine2_kernel,
        out_shape=(shaped(3, 4, 4, 8, 128), shaped(2, 3, 8, 128)),
        in_specs=[SSPEC, VSPEC, HSPEC] + [VSPEC] * 3,
        out_specs=(VSPEC,) * 2,
        scratch_shapes=[pltpu.VMEM((3, NL, 4, 8, 128), F32)] * 2
        + [pltpu.VMEM((NL, 4, 15, 8, 128), F32), pltpu.SemaphoreType.DMA],
        compiler_params=PARAMS,
        cost_estimate=cost(10_000_000, 6_000_000),
        name="fine2",
    )(pos, speed, start, m1, own, p1)


def layer_coefs(speed_ref, j, store):
    layers = speed_ref.shape[0]

    def at(i):
        keep = jnp.where(jnp.logical_and(i >= 0, i < layers), 1.0, 0.0).astype(F32)
        k = jnp.clip(i, 0, layers - 1)
        return [speed_ref[k, c] * keep for c in range(3)]
    coarse_coefs(at(j - 1), at(j), at(j + 1), jnp.float32(1.0), store)


def coefs_kernel(speed_ref, coefs):
    def one(j, carry):
        def store(i, x):
            coefs[j, i] = x
        layer_coefs(speed_ref, j, store)
        return carry
    lax.fori_loop(0, speed_ref.shape[0], one, 0, unroll=2)


def sweep_coefs(speed):
    return pl.pallas_call(
        coefs_kernel,
        out_shape=shaped(speed.shape[0], 15, 8, 128),
        in_specs=[VSPEC],
        out_specs=VSPEC,
        compiler_params=PARAMS,
        cost_estimate=cost(3_000_000, 2_400_000),
        name="coefs",
    )(speed)


def window(slab, halo, layers):
    count = min(layers, 2 + 2 * halo)
    return count, jnp.clip(2 * slab - halo, 0, layers - count)


def psi_step(coefs, src, dst, chunk, low, high):
    def some(i, carry):
        for dj in range(chunk):
            j = i * chunk + dj
            new = psi(lambda n: coefs[j, n],
                      [src[j, c] for c in range(3)],
                      [src[j + 1, c] for c in range(3)],
                      [src[j + 2, c] for c in range(3)])
            for c in range(3):
                dst[j + 1, c] = new[c]
        return carry
    lax.fori_loop(low, high, some, 0)


def first_kernel(pos_ref, speed_ref, near_ref, far_ref, out_ref, state, coefs):
    slab = pos_ref[0]
    n_out, at_out = window(slab, 1, speed_ref.shape[0])
    state[...] = jnp.zeros_like(state)
    inner = 2 * slab - at_out
    state[pl.ds(inner + 1, 2)] = far_ref[...]
    for i in range(n_out):
        def store(n, x, i=i):
            coefs[i, n] = x
        layer_coefs(speed_ref, at_out + i, store)
        new = psi(lambda n, i=i: coefs[i, n], *[[state[i + d, c] for c in range(3)] for d in range(3)])
        for c in range(3):
            out_ref[i, c] = new[c]
    out_ref[pl.ds(inner, 2)] = out_ref[pl.ds(inner, 2)] + near_ref[...]


def first_round(pos, speed, near, far):
    return pl.pallas_call(
        first_kernel,
        out_shape=shaped(4, 3, 8, 128),
        in_specs=[SSPEC] + [VSPEC] * 3,
        out_specs=VSPEC,
        scratch_shapes=[pltpu.VMEM((6, 3, 8, 128), F32), pltpu.VMEM((4, 15, 8, 128), F32)],
        compiler_params=PARAMS,
        cost_estimate=cost(1_000_000, 500_000),
        name="round1",
    )(pos, speed, near, far)


def spread(distance, halo, slab, coefs, got_ref, state_a, state_b):
    layers = coefs.shape[0]
    for ref in (state_a, state_b):
        ref[...] = jnp.zeros_like(ref)
    n_in, at_in = window(slab, halo, layers)
    state_a[pl.ds(at_in + 1, n_in)] = got_ref[...]
    src, dst = state_a, state_b
    chunk = 2 if distance == 1 else 4
    for s in range(distance):
        reach = halo + 1 + s
        low = jnp.maximum(2 * slab - reach, 0) // chunk
        high = (jnp.minimum(2 * slab + 2 + reach, layers) + chunk - 1) // chunk
        psi_step(coefs, src, dst, chunk, low, high)
        src, dst = dst, src
    return src, dst


def round_kernel(distance, halo, pos_ref, coefs, own_ref, got_ref, out_ref, state_a, state_b):
    slab = pos_ref[0]
    layers = coefs.shape[0]
    n_in, at_in = window(slab, halo, layers)
    n_out, at_out = window(slab, halo + distance, layers)
    last, _ = spread(distance, halo, slab, coefs, got_ref, state_a, state_b)
    out_ref[...] = last[pl.ds(at_out + 1, n_out)]
    inner = pl.ds(at_in - at_out, n_in)
    out_ref[inner] = out_ref[inner] + own_ref[...]


def power_kernel(steps, coefs, got_ref, out_ref, state_a, state_b):
    layers = coefs.shape[0]
    for ref in (state_a, state_b):
        ref[0] = jnp.zeros((3, 8, 128), F32)
        ref[layers + 1] = jnp.zeros((3, 8, 128), F32)
    state_a[1:layers + 1] = got_ref[...]

    def pair(i, carry):
        psi_step(coefs, state_a, state_b, FULL_CHUNK, 0, layers // FULL_CHUNK)
        psi_step(coefs, state_b, state_a, FULL_CHUNK, 0, layers // FULL_CHUNK)
        return carry
    lax.fori_loop(0, steps // 2, pair, 0)
    out_ref[...] = state_a[1:layers + 1]


def power(steps, coefs, got):
    layers = coefs.shape[0]
    return pl.pallas_call(
        functools.partial(power_kernel, steps),
        out_shape=shaped(layers, 3, 8, 128),
        in_specs=[VSPEC] * 2,
        out_specs=VSPEC,
        scratch_shapes=[pltpu.VMEM((layers + 2, 3, 8, 128), F32)] * 2,
        compiler_params=PARAMS,
        cost_estimate=cost(steps * 2_000_000, 3_000_000),
        name="power",
    )(coefs, got)


def sweep_round(distance, halo, pos, coefs, own, got):
    layers = coefs.shape[0]
    return pl.pallas_call(
        functools.partial(round_kernel, distance, halo),
        out_shape=shaped(min(layers, 2 + 2 * (halo + distance)), 3, 8, 128),
        in_specs=[SSPEC] + [VSPEC] * 3,
        out_specs=VSPEC,
        scratch_shapes=[pltpu.VMEM((layers + 2, 3, 8, 128), F32)] * 2,
        compiler_params=PARAMS,
        cost_estimate=cost(distance * 2_000_000, 3_000_000),
    )(pos, coefs, own, got)


def total_kernel(got_ref, out_ref):
    for i in range(2):
        for c in range(3):
            terms = [got_ref[s, i, c] for s in range(got_ref.shape[0])]
            while len(terms) > 1:
                terms = [a + b for a, b in zip(terms[::2], terms[1::2])] + terms[len(terms) // 2 * 2:]
            out_ref[i, c] = terms[0]


def slab_total(field):
    layers = field.shape[0]
    got = lax.all_to_all(field.reshape(layers // 2, 2, 3, 8, 128), "gz", 0, 0, tiled=True)
    return pl.pallas_call(
        total_kernel,
        out_shape=shaped(2, 3, 8, 128),
        in_specs=[VSPEC],
        out_specs=VSPEC,
        compiler_params=PARAMS,
        cost_estimate=cost(100_000, 430_000),
        name="total",
    )(got)


def base_kernel(relaxed_ref, base_ref, mean_ref, ev, od):
    for zc in range(2):
        for c in range(3):
            w = [[relaxed_ref[c, 2 * zc + dz, k] for k in range(4)] for dz in range(2)]
            lo, hi = [(v[0] + v[1]) + (v[2] + v[3]) for v in w]
            mean = (lo + hi) * 0.125
            mean_ref[zc, c] = mean
            for dz in range(2):
                row0 = (c * 4 + 2 * zc + dz) * 16
                for q in range(2):
                    ev[pl.ds(row0 + q, 8, stride=2), :] = w[dz][2 * q] - mean
                    od[pl.ds(row0 + q, 8, stride=2), :] = w[dz][2 * q + 1] - mean
    both = jnp.concatenate([ev[...], od[...]], axis=1)
    out = jnp.dot(both, lane_parity(True), precision=HI, preferred_element_type=F32)
    base_ref[...] = out.reshape(3, 4, 16, 256)


def output_base(relaxed):
    return pl.pallas_call(
        base_kernel,
        out_shape=(shaped(3, 4, 16, 256), shaped(2, 3, 8, 128)),
        in_specs=[VSPEC],
        out_specs=(VSPEC,) * 2,
        scratch_shapes=[pltpu.VMEM((192, 128), F32)] * 2,
        compiler_params=PARAMS,
        cost_estimate=cost(25_000_000, 400_000),
        name="base",
    )(relaxed)


def last_kernel(pos_ref, base_ref, mean_ref, near_ref, far_ref, out_ref, half_a, half_b):
    first = pos_ref[1] == 1
    row = lax.broadcasted_iota(jnp.int32, (128, 256), 0)
    col = lax.broadcasted_iota(jnp.int32, (128, 256), 1)
    widen = (col // 2 == row).astype(F32)
    coarse = jnp.where(first, mean_ref[...], near_ref[...] + far_ref[...]).reshape(48, 128)
    wide = jnp.dot(coarse, widen, precision=HI, preferred_element_type=F32)
    for n in range(6):
        for h, half in ((0, half_a), (1, half_b)):
            piece = wide[8 * n:8 * n + 8, 128 * h:128 * h + 128]
            for q in range(2):
                half[pl.ds(16 * n + q, 8, stride=2), :] = piece
    for zc in range(2):
        for c in range(3):
            n = 3 * zc + c
            for h, half in ((0, half_a), (1, half_b)):
                piece = half[16 * n:16 * n + 16, :]
                lanes = slice(128 * h, 128 * h + 128)
                for dz in range(2):
                    out_ref[c, 2 * zc + dz, :, lanes] = base_ref[c, 2 * zc + dz, :, lanes] + piece


def sweep_last(pos, base, mean, near, far):
    return pl.pallas_call(
        last_kernel,
        out_shape=shaped(3, 4, 16, 256),
        in_specs=[SSPEC] + [VSPEC] * 4,
        out_specs=VSPEC,
        scratch_shapes=[pltpu.VMEM((96, 128), F32)] * 2,
        compiler_params=PARAMS,
        cost_estimate=cost(2_000_000, 500_000),
        name="last",
    )(pos, base, mean, near, far)


def moved(block, by_t, by_z):
    nt, nz = lax.axis_size("tm"), lax.axis_size("gz")
    route = [
        ((t - by_t) * nz + z - by_z, t * nz + z)
        for t in range(nt) for z in range(nz)
        if 0 <= t - by_t < nt and 0 <= z - by_z < nz
    ]
    return lax.ppermute(block, ("tm", "gz"), route)


def local(c_states, velocity):
    slab = lax.axis_index("gz")
    t = lax.axis_index("tm")
    slabs = lax.axis_size("gz")
    depth = slabs * velocity.shape[1]
    pos = jnp.stack([slab, (t == 0).astype(jnp.int32), jnp.int32(depth)])
    own = split_fields(c_states[0], velocity)
    start, after, velocity_ext, share = fine1(pos, moved(own, 0, 1), own, moved(own, 0, -1), slabs)
    around = []
    for by in (1, 0, -1):
        around.append(moved(after, 1, by))
    speed = lax.all_to_all(share, "gz", 0, 0, tiled=True)
    relaxed, state = fine2(pos, velocity_ext, start, *around)
    base, mean = output_base(relaxed)
    speed = speed.reshape(2 * slabs, 3, 8, 128)
    coefs = sweep_coefs(speed)
    state = first_round(pos, speed, moved(state, 1, 0), moved(state, 2, 0))
    for distance in (2, 4, 8):
        state = sweep_round(distance, distance - 1, pos, coefs, state, moved(state, distance, 0))
    near = slab_total(state)
    state = power(16, coefs, state)
    near, state = lax.optimization_barrier((near, state))
    far = slab_total(state)
    far = moved(far, 16, 0)
    out = sweep_last(pos, base, mean, near, far)
    return out[None]


def solution(mesh):
    return jax.shard_map(
        local,
        mesh=mesh,
        in_specs=(P("tm", None, "gz", None, None), P(None, "gz", None, None)),
        out_specs=P("tm", None, "gz", None, None),
        check_vma=False,
    )
```

```python
import functools
import jax
import jax.numpy as jnp
from jax import lax
from jax.experimental import pallas as pl
from jax.experimental.pallas import tpu as pltpu
from jax.sharding import PartitionSpec as P


STEPS = 4
KAPPA = 0.04
FINE_UNROLL = True
F32 = jnp.float32
HI = lax.Precision.HIGHEST
VM = pltpu.MemorySpace.VMEM


def lane_parity(transpose=False):
    row = lax.broadcasted_iota(jnp.int32, (256, 256), 1 if transpose else 0)
    col = lax.broadcasted_iota(jnp.int32, (256, 256), 0 if transpose else 1)
    want = 2 * (col % 128) + col // 128
    return (row == want).astype(F32)


def shift(v, by, axis, masked_at, index):
    return jnp.where(index == masked_at, 0.0, pltpu.roll(v, by % v.shape[axis], axis))


def stencil_terms(low, high, mid, inside):
    a = [KAPPA + jnp.maximum(mid[d], 0.0) for d in range(3)]
    b = [KAPPA - jnp.minimum(mid[d], 0.0) for d in range(3)]
    centre = 1.0 - (a[0] + b[0] + a[1] + b[1] + a[2] + b[2])
    m = [[(high[e][c] - low[e][c]) * 0.5 for e in range(3)] for c in range(3)]
    for c in range(3):
        m[c][c] = m[c][c] + centre
    a = [x * inside for x in a]
    b = [x * inside for x in b]
    m = [[x * inside for x in row] for row in m]
    return a, b, m


def iotas():
    sub = lax.broadcasted_iota(jnp.int32, (8, 128), 0)
    lane = lax.broadcasted_iota(jnp.int32, (8, 128), 1)
    return sub, lane


def coarse_coefs(below, here, above, inside, store):
    sub, lane = iotas()
    low = [below, [shift(v, 1, 0, 0, sub) for v in here], [shift(v, 1, 1, 0, lane) for v in here]]
    high = [above, [shift(v, -1, 0, 7, sub) for v in here], [shift(v, -1, 1, 127, lane) for v in here]]
    a, b, m = stencil_terms(low, high, here, inside)
    a[1] = jnp.where(sub == 0, 0.0, a[1])
    b[1] = jnp.where(sub == 7, 0.0, b[1])
    a[2] = jnp.where(lane == 0, 0.0, a[2])
    b[2] = jnp.where(lane == 127, 0.0, b[2])
    flat = a + b + m[0] + m[1] + m[2]
    for i, x in enumerate(flat):
        store(i, x)


def psi(coef, below, here, above):
    a = [coef(i) for i in range(3)]
    b = [coef(3 + i) for i in range(3)]
    out = []
    for c in range(3):
        w = here[c]
        acc = a[0] * below[c] + b[0] * above[c]
        acc = acc + (a[1] * pltpu.roll(w, 1, 0) + b[1] * pltpu.roll(w, 7, 0))
        acc = acc + (a[2] * pltpu.roll(w, 1, 1) + b[2] * pltpu.roll(w, 127, 1))
        acc = acc + (coef(6 + 3 * c) * here[0] + coef(7 + 3 * c) * here[1] + coef(8 + 3 * c) * here[2])
        out.append(acc)
    return out


NL = 12
VSPEC = pl.BlockSpec(memory_space=VM)
HSPEC = pl.BlockSpec(memory_space=pltpu.MemorySpace.HBM)
SSPEC = pl.BlockSpec(memory_space=pltpu.MemorySpace.SMEM)
PARAMS = pltpu.CompilerParams(vmem_limit_bytes=16 << 20)


def shaped(*dims):
    return jax.ShapeDtypeStruct(dims, F32)


def cost(flops, moved):
    return pl.CostEstimate(flops=flops, bytes_accessed=moved, transcendentals=0)


def march4(coefs, first, second):
    src, dst = first, second
    for k in range(1, STEPS + 1):
        def layer(l, carry, src=src, dst=dst):
            w = [[src[c, l, k] for k in range(4)] for c in range(3)]
            for q in range(2):
                for p in range(2):
                    k = 2 * q + p
                    kx = 2 * (1 - q) + p
                    ky = 2 * q + 1 - p
                    cf = [coefs[l, k, i] for i in range(15)]
                    for c in range(3):
                        xo = w[c][kx]
                        xr = pltpu.roll(xo, 7 if q else 1, 0)
                        yo = w[c][ky]
                        yr = pltpu.roll(yo, 127 if p else 1, 1)
                        acc = cf[0] * src[c, l - 1, k] + cf[3] * src[c, l + 1, k]
                        acc = acc + (cf[1] * (xo if q else xr) + cf[4] * (xr if q else xo))
                        acc = acc + (cf[2] * (yo if p else yr) + cf[5] * (yr if p else yo))
                        acc = acc + (cf[6 + 3 * c] * w[0][k] + cf[7 + 3 * c] * w[1][k] + cf[8 + 3 * c] * w[2][k])
                        dst[c, l, k] = acc
            return carry
        lax.fori_loop(k, NL - k, layer, 0, unroll=FINE_UNROLL)
        src, dst = dst, src


def restrict(src, j):
    out = []
    for c in range(3):
        lo = (src[c, 2 * j, 0] + src[c, 2 * j, 1]) + (src[c, 2 * j, 2] + src[c, 2 * j, 3])
        hi = (src[c, 2 * j + 1, 0] + src[c, 2 * j + 1, 1]) + (src[c, 2 * j + 1, 2] + src[c, 2 * j + 1, 3])
        out.append((lo + hi) * 0.125)
    return out


def fine_coefs(slab, depth, speed, coefs):
    sub, lane = iotas()

    def build(l, carry):
        z = slab * 4 + l - 4
        inside = jnp.where(jnp.logical_and(z >= 0, z < depth), 1.0, 0.0).astype(F32)
        mid = [[speed[c, l, k] for c in range(3)] for k in range(4)]
        for q in range(2):
            for p in range(2):
                k = 2 * q + p
                here = mid[k]
                xo = mid[2 * (1 - q) + p]
                yo = mid[2 * q + 1 - p]
                low_z = [speed[c, l - 1, k] for c in range(3)]
                high_z = [speed[c, l + 1, k] for c in range(3)]
                low_x = xo if q else [shift(v, 1, 0, 0, sub) for v in xo]
                high_x = [shift(v, -1, 0, 7, sub) for v in xo] if q else xo
                low_y = yo if p else [shift(v, 1, 1, 0, lane) for v in yo]
                high_y = [shift(v, -1, 1, 127, lane) for v in yo] if p else yo
                a, b, m = stencil_terms([low_z, low_x, low_y], [high_z, high_x, high_y], here, inside)
                if q:
                    b[1] = jnp.where(sub == 7, 0.0, b[1])
                else:
                    a[1] = jnp.where(sub == 0, 0.0, a[1])
                if p:
                    b[2] = jnp.where(lane == 127, 0.0, b[2])
                else:
                    a[2] = jnp.where(lane == 0, 0.0, a[2])
                for i, x in enumerate(a + b + m[0] + m[1] + m[2]):
                    coefs[l, k, i] = x
        return carry

    lax.fori_loop(1, NL - 1, build, 0)


def split_kernel(c_ref, u_ref, out_ref, ev, od):
    perm = lane_parity()
    for part, ref in ((0, c_ref), (1, u_ref)):
        both = jnp.dot(ref[...].reshape(192, 256), perm, precision=HI, preferred_element_type=F32)
        ev[part] = both[:, :128]
        od[part] = both[:, 128:]
        for q in range(2):
            for p, half in ((0, ev), (1, od)):
                got = half[part, pl.ds(q, 96, stride=2), :]
                out_ref[3 * part:3 * part + 3, :, 2 * q + p] = got.reshape(3, 4, 8, 128)


def split_fields(c, u):
    return pl.pallas_call(
        split_kernel,
        out_shape=shaped(6, 4, 4, 8, 128),
        in_specs=[VSPEC] * 2,
        out_specs=VSPEC,
        scratch_shapes=[pltpu.VMEM((2, 192, 128), F32)] * 2,
        compiler_params=PARAMS,
        cost_estimate=cost(50_000_000, 800_000),
        name="split",
    )(c, u)


def fine1_kernel(pos_ref, m1_ref, own_ref, p1_ref, start_ref, after_ref, speed, share_ref,
                 state_a, state_b, begin, coefs, share, sems):
    slab = pos_ref[0]
    depth = pos_ref[2]
    for i, ref in enumerate((m1_ref, own_ref, p1_ref)):
        state_a[:, 4 * i:4 * i + 4] = ref[0:3]
        begin[:, 4 * i:4 * i + 4] = ref[0:3]
        speed[:, 4 * i:4 * i + 4] = ref[3:6]
    keep = pltpu.make_async_copy(begin, start_ref, sems.at[0])
    keep.start()
    for j in (2, 3):
        for c, v in enumerate(restrict(speed, j)):
            for to in range(share.shape[0]):
                share[to, j - 2, c] = 2.0 * v
    send = pltpu.make_async_copy(share, share_ref, sems.at[1])
    send.start()
    fine_coefs(slab, depth, speed, coefs)
    march4(coefs, state_a, state_b)
    after_ref[...] = state_a[:, 4:8]
    keep.wait()
    send.wait()


def fine1(pos, m1, own, p1, slabs):
    return pl.pallas_call(
        fine1_kernel,
        out_shape=(shaped(3, NL, 4, 8, 128), shaped(3, 4, 4, 8, 128), shaped(3, NL, 4, 8, 128),
                   shaped(slabs, 2, 3, 8, 128)),
        in_specs=[SSPEC] + [VSPEC] * 3,
        out_specs=(HSPEC, VSPEC, VSPEC, HSPEC),
        scratch_shapes=[pltpu.VMEM((3, NL, 4, 8, 128), F32)] * 3 + [pltpu.VMEM((NL, 4, 15, 8, 128), F32)]
        + [pltpu.VMEM((slabs, 2, 3, 8, 128), F32), pltpu.SemaphoreType.DMA((2,))],
        compiler_params=PARAMS,
        cost_estimate=cost(10_000_000, 6_000_000),
        name="fine1",
    )(pos, m1, own, p1)


def fine2_kernel(pos_ref, speed, start_ref, m1_ref, own_ref, p1_ref, relaxed_ref, forcing_ref, state_a, state_b, coefs, sem):
    slab = pos_ref[0]
    first = pos_ref[1] == 1
    depth = pos_ref[2]
    @pl.when(first)
    def _():
        fetch = pltpu.make_async_copy(start_ref, state_a, sem)
        fetch.start()
        fetch.wait()

    @pl.when(jnp.logical_not(first))
    def _():
        for i, ref in enumerate((m1_ref, own_ref, p1_ref)):
            state_a[:, 4 * i:4 * i + 4] = ref[...]
    relaxed_ref[...] = state_a[:, 4:8]
    fine_coefs(slab, depth, speed, coefs)
    coarse = {j: restrict(state_a, j) for j in range(1, 5)}
    speed_c = {j: [2.0 * v for v in restrict(speed, j)] for j in range(1, 5)}
    image = {}
    for j in (2, 3):
        cc = {}
        coarse_coefs(*[speed_c[i] for i in (j - 1, j, j + 1)], jnp.float32(1.0), cc.__setitem__)
        image[j] = psi(cc.__getitem__, coarse[j - 1], coarse[j], coarse[j + 1])
    march4(coefs, state_a, state_b)
    for i, j in enumerate((2, 3)):
        again = restrict(state_a, j)
        for c in range(3):
            forcing = again[c] - image[j][c]
            forcing = forcing + jnp.where(first, image[j][c], 0.0)
            forcing_ref[i, c] = forcing


def fine2(pos, speed, start, m1, own, p1):
    return pl.pallas_call(
        fine2_kernel,
        out_shape=(shaped(3, 4, 4, 8, 128), shaped(2, 3, 8, 128)),
        in_specs=[SSPEC, VSPEC, HSPEC] + [VSPEC] * 3,
        out_specs=(VSPEC,) * 2,
        scratch_shapes=[pltpu.VMEM((3, NL, 4, 8, 128), F32)] * 2
        + [pltpu.VMEM((NL, 4, 15, 8, 128), F32), pltpu.SemaphoreType.DMA],
        compiler_params=PARAMS,
        cost_estimate=cost(10_000_000, 6_000_000),
        name="fine2",
    )(pos, speed, start, m1, own, p1)


def layer_coefs(speed_ref, j, store):
    layers = speed_ref.shape[0]

    def at(i):
        keep = jnp.where(jnp.logical_and(i >= 0, i < layers), 1.0, 0.0).astype(F32)
        k = jnp.clip(i, 0, layers - 1)
        return [speed_ref[k, c] * keep for c in range(3)]
    coarse_coefs(at(j - 1), at(j), at(j + 1), jnp.float32(1.0), store)


def coefs_kernel(speed_ref, coefs):
    def one(j, carry):
        def store(i, x):
            coefs[j, i] = x
        layer_coefs(speed_ref, j, store)
        return carry
    lax.fori_loop(0, speed_ref.shape[0], one, 0, unroll=2)


def sweep_coefs(speed):
    return pl.pallas_call(
        coefs_kernel,
        out_shape=shaped(speed.shape[0], 15, 8, 128),
        in_specs=[VSPEC],
        out_specs=VSPEC,
        compiler_params=PARAMS,
        cost_estimate=cost(3_000_000, 2_400_000),
        name="coefs",
    )(speed)


def window(slab, halo, layers):
    count = min(layers, 2 + 2 * halo)
    return count, jnp.clip(2 * slab - halo, 0, layers - count)


def psi_step(coefs, src, dst, chunk, low, high):
    def some(i, carry):
        for dj in range(chunk):
            j = i * chunk + dj
            new = psi(lambda n: coefs[j, n],
                      [src[j, c] for c in range(3)],
                      [src[j + 1, c] for c in range(3)],
                      [src[j + 2, c] for c in range(3)])
            for c in range(3):
                dst[j + 1, c] = new[c]
        return carry
    lax.fori_loop(low, high, some, 0)


def first_kernel(pos_ref, speed_ref, near_ref, far_ref, out_ref, state, coefs):
    slab = pos_ref[0]
    n_out, at_out = window(slab, 1, speed_ref.shape[0])
    state[...] = jnp.zeros_like(state)
    inner = 2 * slab - at_out
    state[pl.ds(inner + 1, 2)] = far_ref[...]
    for i in range(n_out):
        def store(n, x, i=i):
            coefs[i, n] = x
        layer_coefs(speed_ref, at_out + i, store)
        new = psi(lambda n, i=i: coefs[i, n], *[[state[i + d, c] for c in range(3)] for d in range(3)])
        for c in range(3):
            out_ref[i, c] = new[c]
    out_ref[pl.ds(inner, 2)] = out_ref[pl.ds(inner, 2)] + near_ref[...]


def first_round(pos, speed, near, far):
    return pl.pallas_call(
        first_kernel,
        out_shape=shaped(4, 3, 8, 128),
        in_specs=[SSPEC] + [VSPEC] * 3,
        out_specs=VSPEC,
        scratch_shapes=[pltpu.VMEM((6, 3, 8, 128), F32), pltpu.VMEM((4, 15, 8, 128), F32)],
        compiler_params=PARAMS,
        cost_estimate=cost(1_000_000, 500_000),
        name="round1",
    )(pos, speed, near, far)


def power_steps(coefs, state_a, state_b, steps):
    layers = coefs.shape[0]

    def pair(i, carry):
        psi_step(coefs, state_a, state_b, layers, 0, 1)
        psi_step(coefs, state_b, state_a, layers, 0, 1)
        return carry
    lax.fori_loop(0, steps // 2, pair, 0)


def spread(distance, halo, slab, coefs, got_ref, state_a, state_b):
    layers = coefs.shape[0]
    state_a[...] = jnp.zeros_like(state_a)
    state_b[0] = jnp.zeros((3, 8, 128), F32)
    state_b[layers + 1] = jnp.zeros((3, 8, 128), F32)
    n_in, at_in = window(slab, halo, layers)
    state_a[pl.ds(at_in + 1, n_in)] = got_ref[...]
    power_steps(coefs, state_a, state_b, distance)


def round_kernel(distance, halo, pos_ref, coefs, own_ref, got_ref, out_ref, state_a, state_b):
    slab = pos_ref[0]
    layers = coefs.shape[0]
    n_in, at_in = window(slab, halo, layers)
    n_out, at_out = window(slab, halo + distance, layers)
    spread(distance, halo, slab, coefs, got_ref, state_a, state_b)
    out_ref[...] = state_a[pl.ds(at_out + 1, n_out)]
    inner = pl.ds(at_in - at_out, n_in)
    out_ref[inner] = out_ref[inner] + own_ref[...]


def final_kernel(distance, halo, pos_ref, coefs, own_ref, got_ref, share_ref, state_a, state_b):
    slab = pos_ref[0]
    layers = coefs.shape[0]
    n_in, at_in = window(slab, halo, layers)
    spread(distance, halo, slab, coefs, got_ref, state_a, state_b)
    inner = pl.ds(at_in + 1, n_in)
    state_a[inner] = state_a[inner] + own_ref[...]
    share_ref[:, 0] = state_a[1:layers + 1].reshape(layers // 2, 2, 3, 8, 128)
    power_steps(coefs, state_a, state_b, 2 * distance)
    share_ref[:, 1] = state_a[1:layers + 1].reshape(layers // 2, 2, 3, 8, 128)


def sweep_round(distance, halo, final, pos, coefs, own, got):
    layers = coefs.shape[0]
    out = shaped(layers // 2, 2, 2, 3, 8, 128) if final else shaped(min(layers, 2 + 2 * (halo + distance)), 3, 8, 128)
    return pl.pallas_call(
        functools.partial(final_kernel if final else round_kernel, distance, halo),
        out_shape=out,
        in_specs=[SSPEC] + [VSPEC] * 3,
        out_specs=VSPEC,
        scratch_shapes=[pltpu.VMEM((layers + 2, 3, 8, 128), F32)] * 2,
        compiler_params=PARAMS,
        cost_estimate=cost((3 if final else 1) * distance * 2_000_000, 3_000_000),
    )(pos, coefs, own, got)


def total_kernel(got_ref, near_ref, far_ref):
    for i in range(2):
        for c in range(3):
            for part, ref in ((0, near_ref), (1, far_ref)):
                terms = [got_ref[s, part, i, c] for s in range(got_ref.shape[0])]
                while len(terms) > 1:
                    terms = [a + b for a, b in zip(terms[::2], terms[1::2])] + terms[len(terms) // 2 * 2:]
                ref[i, c] = terms[0]


def totals(got):
    return pl.pallas_call(
        total_kernel,
        out_shape=(shaped(2, 3, 8, 128),) * 2,
        in_specs=[VSPEC],
        out_specs=(VSPEC,) * 2,
        compiler_params=PARAMS,
        cost_estimate=cost(200_000, 850_000),
        name="totals",
    )(got)


def base_kernel(relaxed_ref, base_ref, mean_ref, ev, od):
    for zc in range(2):
        for c in range(3):
            w = [[relaxed_ref[c, 2 * zc + dz, k] for k in range(4)] for dz in range(2)]
            lo, hi = [(v[0] + v[1]) + (v[2] + v[3]) for v in w]
            mean = (lo + hi) * 0.125
            mean_ref[zc, c] = mean
            for dz in range(2):
                row0 = (c * 4 + 2 * zc + dz) * 16
                for q in range(2):
                    ev[pl.ds(row0 + q, 8, stride=2), :] = w[dz][2 * q] - mean
                    od[pl.ds(row0 + q, 8, stride=2), :] = w[dz][2 * q + 1] - mean
    both = jnp.concatenate([ev[...], od[...]], axis=1)
    out = jnp.dot(both, lane_parity(True), precision=HI, preferred_element_type=F32)
    base_ref[...] = out.reshape(3, 4, 16, 256)


def output_base(relaxed):
    return pl.pallas_call(
        base_kernel,
        out_shape=(shaped(3, 4, 16, 256), shaped(2, 3, 8, 128)),
        in_specs=[VSPEC],
        out_specs=(VSPEC,) * 2,
        scratch_shapes=[pltpu.VMEM((192, 128), F32)] * 2,
        compiler_params=PARAMS,
        cost_estimate=cost(25_000_000, 400_000),
        name="base",
    )(relaxed)


def last_kernel(pos_ref, base_ref, mean_ref, near_ref, far_ref, out_ref, half_a, half_b):
    first = pos_ref[1] == 1
    row = lax.broadcasted_iota(jnp.int32, (128, 256), 0)
    col = lax.broadcasted_iota(jnp.int32, (128, 256), 1)
    widen = (col // 2 == row).astype(F32)
    coarse = jnp.where(first, mean_ref[...], near_ref[...] + far_ref[...]).reshape(48, 128)
    wide = jnp.dot(coarse, widen, precision=HI, preferred_element_type=F32)
    for n in range(6):
        for h, half in ((0, half_a), (1, half_b)):
            piece = wide[8 * n:8 * n + 8, 128 * h:128 * h + 128]
            for q in range(2):
                half[pl.ds(16 * n + q, 8, stride=2), :] = piece
    for zc in range(2):
        for c in range(3):
            n = 3 * zc + c
            for h, half in ((0, half_a), (1, half_b)):
                piece = half[16 * n:16 * n + 16, :]
                lanes = slice(128 * h, 128 * h + 128)
                for dz in range(2):
                    out_ref[c, 2 * zc + dz, :, lanes] = base_ref[c, 2 * zc + dz, :, lanes] + piece


def sweep_last(pos, base, mean, near, far):
    return pl.pallas_call(
        last_kernel,
        out_shape=shaped(3, 4, 16, 256),
        in_specs=[SSPEC] + [VSPEC] * 4,
        out_specs=VSPEC,
        scratch_shapes=[pltpu.VMEM((96, 128), F32)] * 2,
        compiler_params=PARAMS,
        cost_estimate=cost(2_000_000, 500_000),
        name="last",
    )(pos, base, mean, near, far)


def moved(block, by_t, by_z):
    nt, nz = lax.axis_size("tm"), lax.axis_size("gz")
    route = [
        ((t - by_t) * nz + z - by_z, t * nz + z)
        for t in range(nt) for z in range(nz)
        if 0 <= t - by_t < nt and 0 <= z - by_z < nz
    ]
    return lax.ppermute(block, ("tm", "gz"), route)


def local(c_states, velocity):
    slab = lax.axis_index("gz")
    t = lax.axis_index("tm")
    slabs = lax.axis_size("gz")
    depth = slabs * velocity.shape[1]
    pos = jnp.stack([slab, (t == 0).astype(jnp.int32), jnp.int32(depth)])
    own = split_fields(c_states[0], velocity)
    start, after, velocity_ext, share = fine1(pos, moved(own, 0, 1), own, moved(own, 0, -1), slabs)
    around = []
    for by in (1, 0, -1):
        around.append(moved(after, 1, by))
    speed = lax.all_to_all(share, "gz", 0, 0, tiled=True)
    relaxed, state = fine2(pos, velocity_ext, start, *around)
    base, mean = output_base(relaxed)
    speed = speed.reshape(2 * slabs, 3, 8, 128)
    coefs = sweep_coefs(speed)
    two_back = moved(state, 2, 0)
    one_back = moved(state, 1, 0)
    state = first_round(pos, speed, one_back, two_back)
    for distance in (2, 4, 8):
        state = sweep_round(distance, distance - 1, distance == 8, pos, coefs, state, moved(state, distance, 0))
    near, far = totals(lax.all_to_all(state, "gz", 0, 0, tiled=True))
    out = sweep_last(pos, base, mean, near, moved(far, 16, 0))
    return out[None]


def solution(mesh):
    return jax.shard_map(
        local,
        mesh=mesh,
        in_specs=(P("tm", None, "gz", None, None), P(None, "gz", None, None)),
        out_specs=P("tm", None, "gz", None, None),
        check_vma=False,
    )
```
